128 devices in a mesh: blk: 8 (over x, z_hi), grp: 16 (over z_lo, y, core).
Axes of the slice: x: 4, y: 4, z: 4 (z_hi: 2, z_lo: 2; z = z_hi * 2 + z_lo), core: 2. Of those that a mesh axis runs over, the one named last changes fastest.
Arguments:
- incident: float32 [8, 16384, 240], P('blk', 'grp'), may hold values from -6 to 6
- mie_coef: float32 [8, 16384, 240], P('blk', 'grp'), may hold values from 0.15 to 0.45
- owner_dev: int32 [8, 49152, 1], P('blk', 'grp'), may hold values from 0 to 15; in each aligned block of 3072 rows (0 to 3071, 3072 to 6143, ..., all dimensions but the last counted through in order) at most 512 rows name the same one
- near_row: int32 [8, 49152], P('blk', 'grp'), may hold values from 0 to 1023
- table_id: int32 [8, 49152], P('blk', 'grp'), may hold values from 0 to 7
- tables: bfloat16 [8, 240, 240], replicated, may hold values from -0.4 to 0.6
- wave_out: bfloat16 [240, 512], replicated, may hold values from -0.375 to 0.375
- wave_in: bfloat16 [512, 240], replicated, may hold values from -0.25 to 0.25
- plane_angle: bfloat16 [8, 16384, 512], P('blk', 'grp'), may hold values from -3.140625 to 3.140625
- far_trans: float32 [8, 16, 8, 512], P('blk', 'grp'), may hold values from -0.0625 to 0.0625
Outputs:
- solution: float32 [8, 16384, 240], P('blk', 'grp')
- residual: float32 [8, 16384, 240], P('blk', 'grp')
- hessenberg: float32 [3, 2], replicated
The draws below stay inside these ranges and needn't reach their ends.
Inputs may be any that keep to these rules, and one draw needn't show every extreme that they name: `owner_dev`: among the 3072 requests of one device, at most 512 name the same owner, and some device reaches 512.
All inputs are finite; a program needn't handle non-finite values.
Results may differ from the reference program's by a relative error of at most 0.0075.
Values may be sent and summed in bfloat16 or wider, within the bound.
A program may use at most 128 MiB of HBM per device.

```python
import math
import jax
import jax.numpy as jnp
import numpy as np
from jax import lax

C = 240
M = 512
NTAB = 8
K = 3
P_SIZE = 1024
CAP = 512
Q = 3072
GROUP_ROWS = 16384
GROUP_REQ = 49152
N_BLK = 8
N_GRP = 16


def draw_incident(key, part):
    key_common = jax.random.fold_in(key, 11)
    key_noise = jax.random.fold_in(key, 12)
    total_rows = N_BLK * GROUP_ROWS
    position = jnp.arange(total_rows, dtype=jnp.int32).astype(jnp.float32) / (1.0 * (total_rows - 1))
    position = position.reshape(N_BLK, GROUP_ROWS, 1)
    common = jax.random.normal(key_common, (1, 1, C), jnp.float32)
    noise = 0.5 * jax.random.normal(key_noise, (N_BLK, GROUP_ROWS, C), jnp.float32)
    ramp = 0.4 + 1.2 * position
    return jnp.clip(ramp * (common + noise), -6.0, 6.0)


def draw_mie_coef(key, part):
    key_mie = jax.random.fold_in(key, 21)
    unit = jax.random.uniform(key_mie, (N_BLK, GROUP_ROWS, C), jnp.float32, -1.0, 1.0)
    return 0.3 + 0.15 * unit


def draw_tables(key, part):
    key_shared = jax.random.fold_in(key, 31)
    key_own = jax.random.fold_in(key, 32)
    shared = jax.random.normal(key_shared, (C, C), jnp.float32)
    own = jax.random.normal(key_own, (NTAB, C, C), jnp.float32)
    symmetric = (shared + shared.T) * (0.25 / math.sqrt(2.0 * C))
    identity = jnp.eye(C, dtype=jnp.float32)
    tables = 0.3 * identity[None] + symmetric[None] + own * (0.5 / math.sqrt(1.0 * C))
    return jnp.clip(tables, -0.4, 0.6).astype(jnp.bfloat16)


def plant(drawn, rng, low, high):
    dims = drawn.shape
    spot = [jax.random.randint(jax.random.fold_in(rng, axis), (), 0, dims[axis]) for axis in range(len(dims))]
    drawn = drawn.at[tuple(spot)].set(low)
    longest = dims.index(max(dims))
    spot[longest] = (spot[longest] + 1) % dims[longest]
    return drawn.at[tuple(spot)].set(high)


def levels(own_key, extent, shards, least, top_value):
    gain, own = 1.0, jax.random.fold_in(own_key, 6)
    for dim, parts in shards:
        steps = jnp.exp(jax.random.uniform(jax.random.fold_in(own, dim), (parts,), jnp.float32, least / len(shards), top_value / len(shards)))
        gain = gain * jnp.repeat(steps, extent[dim] // parts).reshape([-1 if axis == dim else 1 for axis in range(len(extent))])
    return gain


def assign_block(stream_key, own, number, rows, amount, top, most, lean):
    order = jax.random.permutation(stream_key, amount)
    heavy_load, usual = shares(amount, rows * top, most, lean, True), shares(amount, rows * top, most, lean, False)
    places = jnp.arange(amount)

    def named(lengths, rotation):
        used = int((lengths > 0).sum())
        fixed = max(1, used // 4)
        shifted = fixed + (places - fixed + rotation * (used - fixed)) % max(1, amount - fixed)
        return jnp.zeros((amount,), jnp.int32).at[order[jnp.where(places < fixed, places, shifted)]].set(jnp.asarray(lengths, jnp.int32))

    lengths = jnp.where(number % 4 == 0, named(heavy_load, number // 4), named(usual, number - number // 4 - 1))
    mixed = jax.random.permutation(jax.random.fold_in(own, 3), amount)
    donor, taker = mixed[0:amount // 2 * 2:2], mixed[1:amount // 2 * 2:2]
    slack = jnp.minimum(lengths[donor] - 1, most - lengths[taker]) // 2
    slack = jnp.where((donor == order[0]) | (taker == order[0]) | (lengths[taker] == 0), 0, jnp.maximum(slack, 0))
    shifted = jax.random.randint(jax.random.fold_in(own, 4), (amount // 2,), 0, 1 << 20) % (slack + 1)
    lengths = lengths.at[donor].add(-shifted).at[taker].add(shifted)
    members = jnp.searchsorted(jnp.cumsum(lengths), jnp.arange(rows * top), side="right").astype(jnp.int32)
    table = members.reshape(top, rows).T
    table = table[jax.random.permutation(jax.random.fold_in(own, 1), rows)]
    rotation = jax.random.randint(jax.random.fold_in(own, 2), (rows, 1), 0, top)
    return jnp.take_along_axis(table, (jnp.arange(top)[None, :] + rotation) % top, axis=1)


def shares(amount, total, limit, slope, full):
    weights = [(1 << 20) // math.isqrt(grade ** slope) + 1 for grade in range(1, amount + 1)]
    largest = limit if full else min(limit, max(-(-total // amount), total * weights[0] // sum(weights)))
    least = 1 if total - largest >= amount - 1 else 0
    holding, surplus = [largest] + [least] * (amount - 1), total - largest - least * (amount - 1)
    while surplus > 0:
        free = [i for i in range(1, amount) if holding[i] < largest] or [i for i in range(1, amount) if holding[i] < limit]
        mass, budget = sum([weights[i] for i in free]), surplus
        for i in free:
            extra = min(limit - holding[i], max(1, budget * weights[i] // mass), surplus)
            holding[i] = holding[i] + extra
            surplus = surplus - extra
    return np.array(holding)


def gaussian(rng, shape, scale, bound, split=(), held_as=jnp.bfloat16):
    values = scale * jax.random.normal(rng, shape, jnp.float32)
    if split:
        values = values * levels(rng, shape, split, -0.22, 0.18)
    return jnp.clip(values, -bound, bound).astype(held_as)


def setup_inputs(seed: int = 0) -> dict:
    key_of = jax.random.split(jax.random.key(seed), 11)
    incident = draw_incident(jax.random.fold_in(key_of[10], 71), 0)
    mie_coef = draw_mie_coef(jax.random.fold_in(key_of[10], 71), 0)
    owner_dev_keys = jax.random.split(jax.random.fold_in(key_of[2], 1), N_BLK * GROUP_REQ // Q)
    owner_dev_turns = jax.random.permutation(jax.random.fold_in(key_of[2], 3), N_BLK * GROUP_REQ // Q)
    owner_dev = jax.vmap(lambda own, number: assign_block(jax.random.fold_in(key_of[2], 2), own, number, Q, N_GRP, 1, CAP, 2))(owner_dev_keys, owner_dev_turns).reshape((N_BLK, GROUP_REQ, 1))
    near_row = plant(jax.random.randint(key_of[3], (N_BLK, GROUP_REQ), 0, P_SIZE), jax.random.fold_in(key_of[3], 1), 0, P_SIZE - 1).astype(jnp.int32)
    table_id = plant(jax.random.randint(key_of[4], (N_BLK, GROUP_REQ), 0, NTAB), jax.random.fold_in(key_of[4], 1), 0, NTAB - 1).astype(jnp.int32)
    tables = draw_tables(jax.random.fold_in(key_of[10], 71), 0)
    wave_out = gaussian(key_of[6], (C, M), C ** -0.5, 0.375)
    wave_in = gaussian(key_of[7], (M, C), M ** -0.5, 0.25)
    plane_angle = jnp.clip(jax.random.uniform(key_of[8], (N_BLK, GROUP_ROWS, M), jnp.float32, -3.140625, 3.140625), -3.140625, 3.140625).astype(jnp.bfloat16)
    far_trans = gaussian(key_of[9], (N_BLK, N_GRP, N_BLK, M), (P_SIZE * (N_BLK - 1)) ** -0.5, 0.0625, ((0, 8), (1, 16)), jnp.float32)
    return {"incident": incident, "mie_coef": mie_coef, "owner_dev": owner_dev, "near_row": near_row, "table_id": table_id, "tables": tables, "wave_out": wave_out, "wave_in": wave_in, "plane_angle": plane_angle, "far_trans": far_trans}


epsilon = 1e-06

def apply_operator(vector, mie_coef, source_ids, table_id, tables, wave_out, wave_in, cosine, far_trans):
    block_count, group_rows, coef_count = vector.shape
    coded = vector.astype(jnp.bfloat16).astype(jnp.float32)
    flat_coded = coded.reshape(-1, coef_count)
    near_terms = jnp.zeros((block_count, source_ids.shape[1], coef_count), jnp.float32)
    for table_index in range(NTAB):
        translated = jnp.dot(flat_coded, tables[table_index].astype(jnp.float32), precision=lax.Precision.HIGHEST).reshape(vector.shape)
        translated = translated.astype(jnp.bfloat16).astype(jnp.float32)
        fetched = jax.vmap(lambda rows_all, wanted: rows_all[wanted])(translated, source_ids)
        near_terms = near_terms + jnp.where((table_id == table_index)[:, :, None], fetched, 0.0)
    near_field = near_terms.reshape(block_count, group_rows, K, coef_count).sum(axis=2)
    outgoing = jnp.dot(flat_coded, wave_out.astype(jnp.float32), precision=lax.Precision.HIGHEST).reshape(block_count, group_rows, M)
    gathered = (cosine * outgoing).reshape(block_count, N_GRP, P_SIZE, M).sum(axis=2)
    far_mask = 1.0 - jnp.eye(block_count, dtype=jnp.float32)
    incoming = jnp.einsum('bgcm,bc,cgm->bgm', far_trans, far_mask, gathered, precision=lax.Precision.HIGHEST)
    spread = (cosine * jnp.repeat(incoming, P_SIZE, axis=1)).astype(jnp.bfloat16).astype(jnp.float32)
    far_field = jnp.dot(spread.reshape(-1, M), wave_in.astype(jnp.float32), precision=lax.Precision.HIGHEST).reshape(vector.shape)
    return vector - mie_coef * (near_field + far_field)

def reference(incident, mie_coef, owner_dev, near_row, table_id, tables, wave_out, wave_in, plane_angle, far_trans):
    source_ids = (owner_dev[:, :, 0] * P_SIZE + near_row).astype(jnp.int32)
    cosine = jnp.cos(plane_angle.astype(jnp.float32))

    def operator(vector):
        return apply_operator(vector, mie_coef, source_ids, table_id, tables, wave_out, wave_in, cosine, far_trans)
    initial_norm = jnp.sqrt(jnp.sum(incident * incident) + epsilon)
    first_basis = incident / initial_norm
    first_image = operator(first_basis)
    diag_first = jnp.sum(first_basis * first_image)
    resid_first = first_image - diag_first * first_basis
    below_first = jnp.sqrt(jnp.sum(resid_first * resid_first) + epsilon)
    second_basis = resid_first / below_first
    second_image = operator(second_basis)
    upper_second = jnp.sum(first_basis * second_image)
    diag_second = jnp.sum(second_basis * second_image)
    resid_second = second_image - upper_second * first_basis - diag_second * second_basis
    below_second = jnp.sqrt(jnp.sum(resid_second * resid_second) + epsilon)
    gram_aa = diag_first * diag_first + below_first * below_first
    gram_ab = diag_first * upper_second + below_first * diag_second
    gram_bb = upper_second * upper_second + diag_second * diag_second + below_second * below_second
    rhs_first = initial_norm * diag_first
    rhs_second = initial_norm * upper_second
    determinant = gram_aa * gram_bb - gram_ab * gram_ab
    coef_first = (gram_bb * rhs_first - gram_ab * rhs_second) / determinant
    coef_second = (gram_aa * rhs_second - gram_ab * rhs_first) / determinant
    solution = coef_first * first_basis + coef_second * second_basis
    residual = incident - coef_first * first_image - coef_second * second_image
    zero_entry = jnp.zeros((), jnp.float32)
    hessenberg = jnp.stack([jnp.stack([diag_first, upper_second]), jnp.stack([below_first, diag_second]), jnp.stack([zero_entry, below_second])])
    return (solution, residual, hessenberg)
```

```python
import functools

import jax
import jax.numpy as jnp
from jax import lax
from jax.experimental import pallas as pl
from jax.experimental.pallas import tpu as pltpu
from jax.sharding import PartitionSpec as P

MESH = pl.DeviceIdType.MESH
F32 = jnp.float32
BF16 = jnp.bfloat16

epsilon = 1e-06

ROWS = 1024
COEF = 240
WAVES = 512
TABLES = 8
PER_ROW = 3
GROUP = 16
BLOCKS = 8
CHUNKS = 8
CHUNK = ROWS // CHUNKS
TILE = 256
UNROLL = 32

Z_FIRST = (True, False, True, False, True, False, True, True)
GO_RIGHT = (True, False, False, True, True, False, False, True)


class Gather:
    def __init__(self, gbuf, send_sems, recv_sems):
        self.gbuf, self.send_sems, self.recv_sems = gbuf, send_sems, recv_sems
        g = lax.axis_index("grp")
        self.z, self.y, self.c = g // 8, (g // 2) % 4, g % 2
        self.me = g
        self.right = self.place(0, 1)
        self.left = self.place(0, 3)
        self.across = self.place(1, 0)
        self.partner = self.place(0, 0, 1)
        self.sent = []

    def place(self, dz, dy, dc=0):
        return ((self.z + dz) % 2) * 8 + ((self.y + dy) % 4) * 2 + (self.c + dc) % 2

    def copy(self, origin, chunk, device, slot):
        rows = pl.ds(pl.multiple_of(origin * ROWS + chunk * CHUNK, CHUNK), CHUNK)
        return pltpu.make_async_remote_copy(
            src_ref=self.gbuf.at[rows],
            dst_ref=self.gbuf.at[rows],
            send_sem=self.send_sems.at[slot],
            recv_sem=self.recv_sems.at[origin, chunk],
            device_id={"grp": device},
            device_id_type=MESH,
        )

    def send(self, origin, chunk, *devices):
        for device in devices:
            copy = self.copy(origin, chunk, device, len(self.sent))
            copy.start()
            self.sent.append(copy)

    def wait(self, origin, chunk):
        self.copy(origin, chunk, self.partner, 0).wait_recv()

    def start(self):
        for k in range(CHUNKS):
            self.send(self.me, k, self.right, self.left, self.across, self.partner)

    def level_one(self):
        for k in range(CHUNKS):
            extra = () if Z_FIRST[k] else (self.across,)
            origin = self.place(0, 3)
            self.wait(origin, k)
            self.send(origin, k, *((self.right,) if GO_RIGHT[k] else ()), *extra, self.partner)
            origin = self.place(0, 1)
            self.wait(origin, k)
            self.send(origin, k, *(() if GO_RIGHT[k] else (self.left,)), *extra, self.partner)
            origin = self.place(1, 0)
            self.wait(origin, k)
            self.send(origin, k, *((self.right, self.left) if Z_FIRST[k] else ()), self.partner)

    def level_two(self):
        for k in range(CHUNKS):
            origin = self.place(0, 2)
            self.wait(origin, k)
            self.send(origin, k, *(() if Z_FIRST[k] else (self.across,)), self.partner)
            origin = self.place(1, 3)
            self.wait(origin, k)
            self.send(origin, k, *((self.right,) if Z_FIRST[k] and GO_RIGHT[k] else ()), self.partner)
            origin = self.place(1, 1)
            self.wait(origin, k)
            self.send(origin, k, *((self.left,) if Z_FIRST[k] and not GO_RIGHT[k] else ()), self.partner)

    def level_three(self):
        for k in range(CHUNKS):
            origin = self.place(1, 2)
            self.wait(origin, k)
            self.send(origin, k, self.partner)

    def finish(self):
        for dz in range(2):
            for dy in (0, 1, 3, 2):
                for k in range(CHUNKS):
                    self.wait(self.place(dz, dy, 1), k)
        for copy in self.sent:
            copy.wait_send()
        self.sent = []


SENDS = CHUNKS * 4 + sum(
    (3 if z else 5) + 1 + (2 if z else 0) + 1 + 3 + (0 if z else 1) + (1 if z else 0) for z in Z_FIRST
)


def shared(buf, send_sems, recv_sems, axis, size, slot):
    copies = []
    for step in range(1, size):
        copy = pltpu.make_async_remote_copy(
            src_ref=buf.at[slot],
            dst_ref=buf.at[slot],
            send_sem=send_sems.at[step - 1],
            recv_sem=recv_sems.at[slot],
            device_id={axis: (slot + step) % size},
            device_id_type=MESH,
        )
        copy.start()
        copies.append(copy)
    return copies


def collect(copies, buf, send_sems, recv_sems, axis, size, slot):
    for step in range(1, size):
        source = (slot + step) % size
        pltpu.make_async_remote_copy(
            src_ref=buf.at[source],
            dst_ref=buf.at[source],
            send_sem=send_sems.at[step - 1],
            recv_sem=recv_sems.at[source],
            device_id={axis: source},
            device_id_type=MESH,
        ).wait_recv()
    for copy in copies:
        copy.wait_send()


def row_of(*values):
    lane = lax.broadcasted_iota(jnp.int32, (1, 128), 1)
    row = jnp.zeros((1, 128), F32)
    for place, value in enumerate(values):
        row = jnp.where(lane == place, value, row)
    return row


def column(rows, place):
    lane = lax.broadcasted_iota(jnp.int32, rows.shape, 1)
    return jnp.sum(jnp.where(lane == place, rows, 0.0), axis=1, keepdims=True)


def total(value):
    return jnp.sum(jnp.sum(value, axis=0, keepdims=True), axis=1, keepdims=True)


def spread_stats(rows):
    squares, inner, left, slope = (column(rows, place) for place in range(4))
    squares_all = jnp.sum(squares, axis=0, keepdims=True)
    inner_all = jnp.sum(inner, axis=0, keepdims=True)
    slope_all = inner_all / jnp.maximum(squares_all, 1e-30)
    gap = slope - slope_all
    left_all = jnp.sum(left + gap * gap * squares, axis=0, keepdims=True)
    return squares_all, inner_all, left_all, slope_all


def kernel(
    source_rows,
    table_ids,
    u_ref,
    mie_ref,
    tables_ref,
    wave_out_ref,
    wave_in_ref,
    angle_ref,
    trans_ref,
    sol_ref,
    res_ref,
    hess_ref,
    gbuf,
    picked,
    ids,
    padded,
    cosine,
    base,
    w1_ref,
    v2_ref,
    w2_ref,
    wbuf,
    stats_a,
    stats_b,
    ag_send,
    ag_recv,
    w_send,
    w_recv,
    a_send,
    a_recv,
    b_send,
    b_recv,
):
    g = lax.axis_index("grp")
    b = lax.axis_index("blk")
    barrier = pltpu.get_barrier_semaphore()
    for step in range(1, GROUP):
        pl.semaphore_signal(barrier, inc=1, device_id={"grp": (g + step) % GROUP}, device_id_type=MESH)
    for step in range(1, BLOCKS):
        pl.semaphore_signal(barrier, inc=1, device_id={"blk": (b + step) % BLOCKS}, device_id_type=MESH)
    pl.semaphore_wait(barrier, GROUP + BLOCKS - 2)

    gather = Gather(gbuf, ag_send, ag_recv)

    def exchange(turn, row, combine):
        stats_a[turn, pl.ds(g, 1)] = row.reshape(1, 1, 128)
        near_buf = stats_a.at[turn]
        copies = shared(near_buf, a_send, a_recv, "grp", GROUP, g)
        collect(copies, near_buf, a_send, a_recv, "grp", GROUP, g)
        row = combine(stats_a[turn].reshape(GROUP, 128))
        stats_b[turn, pl.ds(b, 1)] = row.reshape(1, 1, 128)
        far_buf = stats_b.at[turn]
        copies = shared(far_buf, b_send, b_recv, "blk", BLOCKS, b)
        collect(copies, far_buf, b_send, b_recv, "blk", BLOCKS, b)
        return stats_b[turn].reshape(BLOCKS, 128)

    def prepare():
        padded[...] = jnp.zeros_like(padded)
        for t in range(TABLES):
            padded[t, 0:COEF, :] = tables_ref[t]
        for k in range(PER_ROW):

            @pl.loop(0, ROWS // UNROLL)
            def _(turn):
                for step in range(UNROLL):
                    row = turn * UNROLL + step
                    value = table_ids[row * PER_ROW + k]
                    ids[pl.ds(k * ROWS + row, 1), :] = jnp.full((1, 128), value, jnp.int32).astype(F32)

        @pl.loop(0, ROWS // TILE)
        def _(tile):
            rows = pl.ds(pl.multiple_of(tile * TILE, TILE), TILE)
            cosine[rows, :] = jnp.cos(angle_ref[rows, :].astype(F32))

    def operate(vec_ref, out_ref, first):
        @pl.loop(0, ROWS // TILE)
        def _(tile):
            start = pl.multiple_of(tile * TILE, TILE)
            coded = vec_ref[pl.ds(start, TILE), :].astype(BF16)
            wide = jnp.concatenate([coded, jnp.zeros((TILE, 256 - COEF), BF16)], axis=1)
            gbuf[pl.ds(pl.multiple_of(g * ROWS + start, TILE), TILE)] = wide.reshape(TILE, 2, 128)

        gather.start()
        if first:
            prepare()

        def far_out(tile, wave):
            rows = pl.ds(pl.multiple_of(tile * TILE, TILE), TILE)
            coded = vec_ref[rows, :].astype(BF16)
            outgoing = jnp.dot(coded, wave_out_ref[...], preferred_element_type=F32)
            return wave + jnp.sum(cosine[rows, :] * outgoing, axis=0, keepdims=True)

        wave = lax.fori_loop(0, ROWS // TILE, far_out, jnp.zeros((1, WAVES), F32))
        wbuf[pl.ds(b, 1)] = wave.reshape(1, 1, WAVES)
        wave_copies = shared(wbuf, w_send, w_recv, "blk", BLOCKS, b)
        gather.level_one()
        collect(wave_copies, wbuf, w_send, w_recv, "blk", BLOCKS, b)
        incoming = jnp.zeros((1, WAVES), F32)
        for c in range(BLOCKS):
            term = trans_ref[c : c + 1, :] * wbuf[c]
            incoming = incoming + jnp.where(b == c, jnp.zeros_like(term), term)

        @pl.loop(0, ROWS // TILE)
        def _(tile):
            rows = pl.ds(pl.multiple_of(tile * TILE, TILE), TILE)
            spread = (cosine[rows, :] * incoming).astype(BF16)
            base[rows, :] = jnp.dot(spread, wave_in_ref[...], preferred_element_type=F32)

        gather.level_two()
        gather.level_three()
        gather.finish()

        for k in range(PER_ROW):

            @pl.loop(0, ROWS // UNROLL)
            def _(turn):
                first_row = turn * UNROLL
                places = [source_rows[(first_row + step) * PER_ROW + k] for step in range(UNROLL)]
                values = [gbuf[place].astype(F32) for place in places]
                for step, value in enumerate(values):
                    picked[pl.ds((k * ROWS + first_row + step) * 2, 2), :] = value

        @pl.loop(0, ROWS // TILE)
        def _(tile):
            start = pl.multiple_of(tile * TILE, TILE)
            rows = pl.ds(start, TILE)
            near = jnp.zeros((TILE, COEF), F32)
            for k in range(PER_ROW):
                low = picked[pl.ds(2 * (k * ROWS + start), TILE, 2), :]
                high = picked[pl.ds(2 * (k * ROWS + start) + 1, TILE, 2), :]
                wanted = jnp.concatenate([low, high], axis=1).astype(BF16)
                table = ids[pl.ds(k * ROWS + start, TILE), :]
                table = jnp.concatenate([table, table], axis=1).astype(BF16)
                term = jnp.zeros((TILE, COEF), F32)
                for t in range(TABLES):
                    chosen = jnp.where(table == jnp.asarray(t, BF16), wanted, jnp.zeros_like(wanted))
                    term = term + jnp.dot(chosen, padded[t], preferred_element_type=F32)
                near = near + term.astype(BF16).astype(F32)
            out_ref[rows, :] = vec_ref[rows, :] - mie_ref[rows, :] * (near + base[rows, :])

    def tiles(step, count):
        return lax.fori_loop(0, ROWS // TILE, step, (jnp.zeros((1, 1), F32),) * count)

    def tile_rows(tile):
        return pl.ds(pl.multiple_of(tile * TILE, TILE), TILE)

    operate(u_ref, w1_ref, True)

    def first_sums(tile, sums):
        rows = tile_rows(tile)
        u, w = u_ref[rows, :], w1_ref[rows, :]
        return sums[0] + total(u * u), sums[1] + total(u * w)

    squares, inner = tiles(first_sums, 2)
    slope = inner / jnp.maximum(squares, 1e-30)

    def left_sum(tile, sums):
        rows = tile_rows(tile)
        rest = w1_ref[rows, :] - slope * u_ref[rows, :]
        return (sums[0] + total(rest * rest),)

    (left,) = tiles(left_sum, 1)
    parts = exchange(0, row_of(squares, inner, left, slope), lambda rows: row_of(*spread_stats(rows)))
    squares, inner, left, slope = spread_stats(parts)
    beta_squared = squares + epsilon
    beta = jnp.sqrt(beta_squared)
    h11 = inner / beta_squared
    gap = slope - h11
    h21 = jnp.sqrt((left + gap * gap * squares) / beta_squared + epsilon)
    scale = 1.0 / (beta * h21)

    @pl.loop(0, ROWS // TILE)
    def _(tile):
        rows = tile_rows(tile)
        v2_ref[rows, :] = (w1_ref[rows, :] - h11 * u_ref[rows, :]) * scale

    operate(v2_ref, w2_ref, False)

    def second_sums(tile, sums):
        rows = tile_rows(tile)
        u, v, w = u_ref[rows, :], v2_ref[rows, :], w2_ref[rows, :]
        pairs = (u * w, v * w, w * w, u * v, v * v)
        return tuple(have + total(pair) for have, pair in zip(sums, pairs))

    sums = tiles(second_sums, 5)
    parts = exchange(1, row_of(*sums), lambda rows: jnp.sum(rows, axis=0, keepdims=True))
    uw, vw, ww, uv, vv = (column(jnp.sum(parts, axis=0, keepdims=True), place) for place in range(5))
    h12 = uw / beta
    h22 = vw
    left = ww + h12 * h12 * (squares / beta_squared - 2.0) + h22 * h22 * (vv - 2.0) + 2.0 * h12 * h22 * (uv / beta)
    h32 = jnp.sqrt(jnp.maximum(left, 0.0) + epsilon)
    gram_aa = h11 * h11 + h21 * h21
    gram_ab = h11 * h12 + h21 * h22
    gram_bb = h12 * h12 + h22 * h22 + h32 * h32
    rhs_first = beta * h11
    rhs_second = beta * h12
    determinant = gram_aa * gram_bb - gram_ab * gram_ab
    y1 = (gram_bb * rhs_first - gram_ab * rhs_second) / determinant
    y2 = (gram_aa * rhs_second - gram_ab * rhs_first) / determinant
    y1_scaled = y1 / beta

    @pl.loop(0, ROWS // TILE)
    def _(tile):
        rows = tile_rows(tile)
        u = u_ref[rows, :]
        sol_ref[rows, :] = y1_scaled * u + y2 * v2_ref[rows, :]
        res_ref[rows, :] = u - y1_scaled * w1_ref[rows, :] - y2 * w2_ref[rows, :]

    at_row = lax.broadcasted_iota(jnp.int32, (3, 2), 0)
    at_col = lax.broadcasted_iota(jnp.int32, (3, 2), 1)
    left_col = jnp.where(at_row == 0, h11, jnp.where(at_row == 1, h21, jnp.zeros((3, 2), F32)))
    right_col = jnp.where(at_row == 0, h12, jnp.where(at_row == 1, h22, h32))
    hess_ref[...] = jnp.where(at_col == 0, left_col, right_col)


def body(incident, mie_coef, owner_dev, near_row, table_id, tables, wave_out, wave_in, plane_angle, far_trans):
    source_rows = owner_dev[0, :, 0] * ROWS + near_row[0]
    vmem = pl.BlockSpec(memory_space=pltpu.VMEM)
    smem = pl.BlockSpec(memory_space=pltpu.SMEM)
    dma = pltpu.SemaphoreType.DMA
    sol, res, hess = pl.pallas_call(
        kernel,
        out_shape=(
            jax.ShapeDtypeStruct((ROWS, COEF), F32),
            jax.ShapeDtypeStruct((ROWS, COEF), F32),
            jax.ShapeDtypeStruct((3, 2), F32),
        ),
        in_specs=[smem, smem] + [vmem] * 7,
        out_specs=(vmem, vmem, vmem),
        scratch_shapes=[
            pltpu.VMEM((GROUP * ROWS, 2, 128), BF16),
            pltpu.VMEM((PER_ROW * ROWS * 2, 128), F32),
            pltpu.VMEM((PER_ROW * ROWS, 128), F32),
            pltpu.VMEM((TABLES, 256, COEF), BF16),
            pltpu.VMEM((ROWS, WAVES), F32),
            pltpu.VMEM((ROWS, COEF), F32),
            pltpu.VMEM((ROWS, COEF), F32),
            pltpu.VMEM((ROWS, COEF), F32),
            pltpu.VMEM((ROWS, COEF), F32),
            pltpu.VMEM((BLOCKS, 1, WAVES), F32),
            pltpu.VMEM((2, GROUP, 1, 128), F32),
            pltpu.VMEM((2, BLOCKS, 1, 128), F32),
            dma((SENDS,)),
            dma((GROUP, CHUNKS)),
            dma((BLOCKS - 1,)),
            dma((BLOCKS,)),
            dma((GROUP - 1,)),
            dma((GROUP,)),
            dma((BLOCKS - 1,)),
            dma((BLOCKS,)),
        ],
        compiler_params=pltpu.CompilerParams(
            collective_id=0, has_side_effects=True, vmem_limit_bytes=62 * 2**20
        ),
    )(
        source_rows,
        table_id[0],
        incident[0],
        mie_coef[0],
        tables,
        wave_out,
        wave_in,
        plane_angle[0],
        far_trans[0, 0],
    )
    return sol[None], res[None], hess


def solution(mesh):
    return jax.shard_map(
        body,
        mesh=mesh,
        in_specs=(
            P("blk", "grp", None),
            P("blk", "grp", None),
            P("blk", "grp", None),
            P("blk", "grp"),
            P("blk", "grp"),
            P(),
            P(),
            P(),
            P("blk", "grp", None),
            P("blk", "grp", None, None),
        ),
        out_specs=(P("blk", "grp", None), P("blk", "grp", None), P()),
        check_vma=False,
    )
```

```python
import functools

import jax
import jax.numpy as jnp
from jax import lax
from jax.experimental import pallas as pl
from jax.experimental.pallas import tpu as pltpu
from jax.sharding import PartitionSpec as P

MESH = pl.DeviceIdType.MESH
F32 = jnp.float32
BF16 = jnp.bfloat16

epsilon = 1e-06

ROWS = 1024
COEF = 240
WAVES = 512
TABLES = 8
PER_ROW = 3
GROUP = 16
BLOCKS = 8
CHUNKS = 16
CHUNK = ROWS // CHUNKS
TILE = 256
TILES = ROWS // TILE
UNROLL = 32

Z_FIRST = (True, False, True, False, True, False, True, False, True, False, True, False, True, False, True, True)
GO_RIGHT = (True, True, False, False, True, True, False, False, True, True, False, False, True, False, False, True)


class Gather:
    def __init__(self, gbuf, send_sems, recv_sems):
        self.gbuf, self.send_sems, self.recv_sems = gbuf, send_sems, recv_sems
        g = lax.axis_index("grp")
        self.z, self.y, self.c = g // 8, (g // 2) % 4, g % 2
        self.me = g
        self.right = self.place(0, 1)
        self.left = self.place(0, 3)
        self.across = self.place(1, 0)
        self.partner = self.place(0, 0, 1)
        self.sent = []

    def place(self, dz, dy, dc=0):
        return ((self.z + dz) % 2) * 8 + ((self.y + dy) % 4) * 2 + (self.c + dc) % 2

    def copy(self, origin, chunk, device, slot):
        rows = pl.ds(pl.multiple_of(origin * ROWS + chunk * CHUNK, CHUNK), CHUNK)
        return pltpu.make_async_remote_copy(
            src_ref=self.gbuf.at[rows],
            dst_ref=self.gbuf.at[rows],
            send_sem=self.send_sems.at[slot],
            recv_sem=self.recv_sems.at[origin, chunk],
            device_id={"grp": device},
            device_id_type=MESH,
        )

    def send(self, origin, chunk, *devices):
        for device in devices:
            copy = self.copy(origin, chunk, device, len(self.sent))
            copy.start()
            self.sent.append(copy)

    def wait(self, origin, chunk):
        self.copy(origin, chunk, self.partner, 0).wait_recv()

    def store(self, tile, coded):
        start = pl.multiple_of(self.me * ROWS + tile * TILE, TILE)
        self.gbuf[pl.ds(start, TILE)] = coded.reshape(TILE, 2, 128)

    def start(self, tile):
        for k in range(tile * TILE // CHUNK, (tile + 1) * TILE // CHUNK):
            self.send(self.me, k, self.right, self.left, self.across, self.partner)

    def level_one(self):
        for k in range(CHUNKS):
            extra = () if Z_FIRST[k] else (self.across,)
            origin = self.place(0, 3)
            self.wait(origin, k)
            self.send(origin, k, *((self.right,) if GO_RIGHT[k] else ()), *extra, self.partner)
            origin = self.place(0, 1)
            self.wait(origin, k)
            self.send(origin, k, *(() if GO_RIGHT[k] else (self.left,)), *extra, self.partner)
            origin = self.place(1, 0)
            self.wait(origin, k)
            self.send(origin, k, *((self.right, self.left) if Z_FIRST[k] else ()), self.partner)

    def level_two(self):
        for k in range(CHUNKS):
            origin = self.place(0, 2)
            self.wait(origin, k)
            self.send(origin, k, *(() if Z_FIRST[k] else (self.across,)), self.partner)
            origin = self.place(1, 3)
            self.wait(origin, k)
            self.send(origin, k, *((self.right,) if Z_FIRST[k] and GO_RIGHT[k] else ()), self.partner)
            origin = self.place(1, 1)
            self.wait(origin, k)
            self.send(origin, k, *((self.left,) if Z_FIRST[k] and not GO_RIGHT[k] else ()), self.partner)

    def level_three(self):
        for k in range(CHUNKS):
            origin = self.place(1, 2)
            self.wait(origin, k)
            self.send(origin, k, self.partner)

    def finish(self):
        for dz in range(2):
            for dy in (0, 1, 3, 2):
                for k in range(CHUNKS):
                    self.wait(self.place(dz, dy, 1), k)

    def drain(self):
        for copy in self.sent:
            copy.wait_send()


SENDS = CHUNKS * 15


class Share:
    def __init__(self, buf, send_sems, recv_sems, axis, size):
        self.buf, self.send_sems, self.recv_sems, self.axis, self.size = buf, send_sems, recv_sems, axis, size
        self.slot = lax.axis_index(axis)

    def copy(self, source, target, step):
        return pltpu.make_async_remote_copy(
            src_ref=self.buf.at[source],
            dst_ref=self.buf.at[source],
            send_sem=self.send_sems.at[step - 1],
            recv_sem=self.recv_sems.at[source],
            device_id={self.axis: target},
            device_id_type=MESH,
        )

    def start(self, row):
        self.buf[pl.ds(self.slot, 1)] = row.reshape(1, 1, row.shape[1])
        for step in range(1, self.size):
            self.copy(self.slot, (self.slot + step) % self.size, step).start()

    def finish(self):
        for step in range(1, self.size):
            other = (self.slot + step) % self.size
            self.copy(other, other, step).wait_recv()
        for step in range(1, self.size):
            self.copy(self.slot, (self.slot + step) % self.size, step).wait_send()
        return self.buf[...].reshape(self.size, self.buf.shape[2])


def row_of(*values):
    lane = lax.broadcasted_iota(jnp.int32, (1, 128), 1)
    row = jnp.zeros((1, 128), F32)
    for place, value in enumerate(values):
        row = jnp.where(lane == place, value, row)
    return row


def column(rows, place):
    lane = lax.broadcasted_iota(jnp.int32, rows.shape, 1)
    return jnp.sum(jnp.where(lane == place, rows, 0.0), axis=1, keepdims=True)


def total(value):
    return jnp.sum(jnp.sum(value, axis=0, keepdims=True), axis=1, keepdims=True)


def spread_stats(rows):
    squares, inner, left, slope = (column(rows, place) for place in range(4))
    squares_all = jnp.sum(squares, axis=0, keepdims=True)
    inner_all = jnp.sum(inner, axis=0, keepdims=True)
    slope_all = inner_all / jnp.maximum(squares_all, 1e-30)
    gap = slope - slope_all
    left_all = jnp.sum(left + gap * gap * squares, axis=0, keepdims=True)
    return squares_all, inner_all, left_all, slope_all


def rows_of(tile):
    return pl.ds(pl.multiple_of(tile * TILE, TILE), TILE)


def turned(tall):
    return jnp.concatenate([tall, jnp.zeros((256 - COEF, TILE), tall.dtype)], axis=0).T


def kernel(
    owners,
    near_rows,
    table_ids,
    u_ref,
    mie_hbm,
    tables_hbm,
    wave_out_hbm,
    wave_in_hbm,
    angle_hbm,
    trans_ref,
    b1_hbm,
    q_hbm,
    scal_ref,
    hess_ref,
    gbuf_a,
    gbuf_b,
    places,
    picked,
    ids,
    padded,
    cosine,
    base,
    coded,
    mie,
    mie_tall,
    tables,
    wave_out,
    wave_in,
    wave_in_tall,
    angle,
    b1_tall,
    q_tall,
    wbuf_a,
    wbuf_b,
    stats_a,
    stats_b,
    stats_c,
    stats_d,
    in_sems,
    out_sems,
    aga_send,
    aga_recv,
    agb_send,
    agb_recv,
    wa_send,
    wa_recv,
    wb_send,
    wb_recv,
    a_send,
    a_recv,
    b_send,
    b_recv,
    c_send,
    c_recv,
    d_send,
    d_recv,
):
    g = lax.axis_index("grp")
    b = lax.axis_index("blk")
    barrier = pltpu.get_barrier_semaphore()
    for step in range(1, GROUP):
        pl.semaphore_signal(barrier, inc=1, device_id={"grp": (g + step) % GROUP}, device_id_type=MESH)
    for step in range(1, BLOCKS):
        pl.semaphore_signal(barrier, inc=1, device_id={"blk": (b + step) % BLOCKS}, device_id_type=MESH)

    loads = [
        pltpu.make_async_copy(source, target, in_sems.at[place])
        for place, (source, target) in enumerate(
            (
                (angle_hbm, angle),
                (wave_out_hbm, wave_out),
                (wave_in_hbm, wave_in_tall),
                (mie_hbm, mie_tall),
                (tables_hbm, tables),
            )
        )
    ]
    for load in loads:
        load.start()

    first = Gather(gbuf_a, aga_send, aga_recv)
    second = Gather(gbuf_b, agb_send, agb_recv)
    waves_first = Share(wbuf_a, wa_send, wa_recv, "blk", BLOCKS)
    waves_second = Share(wbuf_b, wb_send, wb_recv, "blk", BLOCKS)
    share_a = Share(stats_a, a_send, a_recv, "grp", GROUP)
    share_b = Share(stats_b, b_send, b_recv, "blk", BLOCKS)
    share_c = Share(stats_c, c_send, c_recv, "grp", GROUP)
    share_d = Share(stats_d, d_send, d_recv, "blk", BLOCKS)

    for tile in range(TILES):
        block = turned(u_ref[:, tile * TILE : (tile + 1) * TILE]).astype(BF16)
        coded[rows_of(tile), :] = block
        first.store(tile, block)
        if tile == 0:
            pl.semaphore_wait(barrier, GROUP + BLOCKS - 2)
        first.start(tile)

    def tall_sums(step, count):
        sums = (jnp.zeros((1, 1), F32),) * count
        for tile in range(TILES):
            sums = step(slice(tile * TILE, (tile + 1) * TILE), sums)
        return sums

    def own_wave():
        def step(tile, wave):
            rows = rows_of(tile)
            outgoing = jnp.dot(coded[rows, 0:COEF], wave_out[...], preferred_element_type=F32)
            return wave + jnp.sum(cosine[rows, :] * outgoing, axis=0, keepdims=True)

        return lax.fori_loop(0, TILES, step, jnp.zeros((1, WAVES), F32))

    def far_field(waves):
        arrived = waves.finish()
        incoming = jnp.zeros((1, WAVES), F32)
        for c in range(BLOCKS):
            term = trans_ref[c : c + 1, :] * arrived[c : c + 1, :]
            incoming = incoming + jnp.where(b == c, jnp.zeros_like(term), term)

        @pl.loop(0, TILES)
        def _(tile):
            rows = rows_of(tile)
            spread = (cosine[rows, :] * incoming).astype(BF16)
            base[rows, :] = jnp.dot(spread, wave_in[...], preferred_element_type=F32)

    def fetch(tile, gbuf):
        for k in range(PER_ROW):

            @pl.loop(0, TILE // UNROLL)
            def _(turn):
                begin = k * ROWS + tile * TILE + turn * UNROLL
                values = [gbuf[places[begin + step]].astype(F32) for step in range(UNROLL)]
                for step, value in enumerate(values):
                    picked[pl.ds((begin + step) * 2, 2), :] = value

    def fields(tile):
        start = tile * TILE
        near = jnp.zeros((TILE, COEF), F32)
        for k in range(PER_ROW):
            low = picked[pl.ds(2 * (k * ROWS + start), TILE, 2), :]
            high = picked[pl.ds(2 * (k * ROWS + start) + 1, TILE, 2), :]
            wanted = jnp.concatenate([low, high], axis=1).astype(BF16)
            table = ids[pl.ds(k * ROWS + start, TILE), :]
            table = jnp.concatenate([table, table], axis=1).astype(BF16)
            term = jnp.zeros((TILE, COEF), F32)
            for t in range(TABLES):
                chosen = jnp.where(table == jnp.asarray(t, BF16), wanted, jnp.zeros_like(wanted))
                term = term + jnp.dot(chosen, padded[t], preferred_element_type=F32)
            near = near + term.astype(BF16).astype(F32)
        rows = rows_of(tile)
        return mie[rows, 0:COEF] * (near + base[rows, :])

    def widened(block):
        return jnp.concatenate([block, jnp.zeros((TILE, 256 - COEF), F32)], axis=1)

    loads[0].wait()

    @pl.loop(0, TILES)
    def _(tile):
        rows = rows_of(tile)
        cosine[rows, :] = jnp.cos(angle[rows, :].astype(F32))

    loads[1].wait()
    waves_first.start(own_wave())
    first.level_one()
    for load in loads[2:]:
        load.wait()
    wave_in[...] = jnp.concatenate(
        [wave_in_tall[...].astype(F32), jnp.zeros((256 - COEF, WAVES), F32)], axis=0
    ).T[:, 0:COEF].astype(BF16)
    far_field(waves_first)
    padded[...] = jnp.zeros_like(padded)
    for t in range(TABLES):
        padded[t, 0:COEF, :] = tables[t]
    for tile in range(TILES):
        mie[rows_of(tile), :] = turned(mie_tall[:, tile * TILE : (tile + 1) * TILE])
    for k in range(PER_ROW):

        @pl.loop(0, ROWS // UNROLL)
        def _(turn):
            for step in range(UNROLL):
                row = turn * UNROLL + step
                request = row * PER_ROW + k
                places[k * ROWS + row] = owners[request] * ROWS + near_rows[request]
                value = jnp.full((1, 128), table_ids[request], jnp.int32).astype(F32)
                ids[pl.ds(k * ROWS + row, 1), :] = value

    def square(cols, sums):
        u = u_ref[:, cols]
        return (sums[0] + total(u * u),)

    (squares,) = tall_sums(square, 1)
    first.level_two()
    first.level_three()
    first.finish()

    for tile in range(TILES):
        fetch(tile, gbuf_a)
        block = widened(fields(tile))
        narrow = block.astype(BF16)
        coded[rows_of(tile), :] = narrow
        second.store(tile, narrow)
        second.start(tile)
        b1_tall[:, tile * TILE : (tile + 1) * TILE] = block.T[0:COEF]

    b1_out = pltpu.make_async_copy(b1_tall, b1_hbm, out_sems.at[0])
    b1_out.start()
    waves_second.start(own_wave())

    def product(cols, sums):
        return (sums[0] + total(u_ref[:, cols] * b1_tall[:, cols]),)

    (inner,) = tall_sums(product, 1)
    slope = inner / jnp.maximum(squares, 1e-30)

    def left_over(cols, sums):
        rest = b1_tall[:, cols] - slope * u_ref[:, cols]
        return (sums[0] + total(rest * rest),)

    (left,) = tall_sums(left_over, 1)
    share_a.start(row_of(squares, inner, left, slope))
    second.level_one()
    share_b.start(row_of(*spread_stats(share_a.finish())))
    far_field(waves_second)
    second.level_two()
    squares, inner, left, slope = spread_stats(share_b.finish())
    beta_squared = squares + epsilon
    beta = jnp.sqrt(beta_squared)
    h11 = (squares - inner) / beta_squared
    rest_first = (inner + epsilon) / beta_squared
    gap = slope - rest_first
    h21 = jnp.sqrt((left + gap * gap * squares) / beta_squared + epsilon)
    scale = 1.0 / (beta * h21)
    second.level_three()
    first.drain()
    second.finish()

    sums = (jnp.zeros((1, 1), F32),) * 5
    for tile in range(TILES):
        fetch(tile, gbuf_b)
        q = widened(fields(tile)).T[0:COEF]
        cols = slice(tile * TILE, (tile + 1) * TILE)
        q_tall[:, cols] = q
        u, b1 = u_ref[:, cols], b1_tall[:, cols]
        v = (rest_first * u - b1) * scale
        w = (rest_first * (u - b1) - (b1 - q)) * scale
        pairs = (u * w, v * w, w * w, u * v, v * v)
        sums = tuple(have + total(pair) for have, pair in zip(sums, pairs))

    share_c.start(row_of(*sums))
    q_out = pltpu.make_async_copy(q_tall, q_hbm, out_sems.at[1])
    q_out.start()
    share_d.start(jnp.sum(share_c.finish(), axis=0, keepdims=True))
    second.drain()
    parts = jnp.sum(share_d.finish(), axis=0, keepdims=True)
    uw, vw, ww, uv, vv = (column(parts, place) for place in range(5))
    h12 = uw / beta
    h22 = vw
    left = ww + h12 * h12 * (squares / beta_squared - 2.0) + h22 * h22 * (vv - 2.0) + 2.0 * h12 * h22 * (uv / beta)
    h32 = jnp.sqrt(jnp.maximum(left, 0.0) + epsilon)
    gram_aa = h11 * h11 + h21 * h21
    gram_ab = h11 * h12 + h21 * h22
    gram_bb = h12 * h12 + h22 * h22 + h32 * h32
    rhs_first = beta * h11
    rhs_second = beta * h12
    determinant = gram_aa * gram_bb - gram_ab * gram_ab
    y1 = (gram_bb * rhs_first - gram_ab * rhs_second) / determinant
    y2 = (gram_aa * rhs_second - gram_ab * rhs_first) / determinant
    scal_ref[...] = row_of(y1 / beta, y2 * scale, rest_first)
    at_row = lax.broadcasted_iota(jnp.int32, (2, 3), 1)
    at_col = lax.broadcasted_iota(jnp.int32, (2, 3), 0)
    left_col = jnp.where(at_row == 0, h11, jnp.where(at_row == 1, h21, jnp.zeros((2, 3), F32)))
    right_col = jnp.where(at_row == 0, h12, jnp.where(at_row == 1, h22, h32))
    hess_ref[...] = jnp.where(at_col == 0, left_col, right_col)
    b1_out.wait()
    q_out.wait()


def body(incident, mie_coef, owner_dev, near_row, table_id, tables, wave_out, wave_in, plane_angle, far_trans):
    vmem = pl.BlockSpec(memory_space=pltpu.VMEM)
    smem = pl.BlockSpec(memory_space=pltpu.SMEM)
    anywhere = pl.BlockSpec(memory_space=pl.ANY)
    dma = pltpu.SemaphoreType.DMA
    u = incident[0].T
    blk_sems = [dma((BLOCKS - 1,)), dma((BLOCKS,))]
    grp_sems = [dma((GROUP - 1,)), dma((GROUP,))]
    b1, q, scal, hess = pl.pallas_call(
        kernel,
        out_shape=(
            jax.ShapeDtypeStruct((COEF, ROWS), F32),
            jax.ShapeDtypeStruct((COEF, ROWS), F32),
            jax.ShapeDtypeStruct((1, 128), F32),
            jax.ShapeDtypeStruct((2, 3), F32),
        ),
        in_specs=[smem, smem, smem, vmem] + [anywhere] * 5 + [vmem],
        out_specs=(anywhere, anywhere, vmem, vmem),
        scratch_shapes=[
            pltpu.VMEM((GROUP * ROWS, 2, 128), BF16),
            pltpu.VMEM((GROUP * ROWS, 2, 128), BF16),
            pltpu.SMEM((PER_ROW * ROWS,), jnp.int32),
            pltpu.VMEM((PER_ROW * ROWS * 2, 128), F32),
            pltpu.VMEM((PER_ROW * ROWS, 128), F32),
            pltpu.VMEM((TABLES, 256, COEF), BF16),
            pltpu.VMEM((ROWS, WAVES), F32),
            pltpu.VMEM((ROWS, COEF), F32),
            pltpu.VMEM((ROWS, 256), BF16),
            pltpu.VMEM((ROWS, 256), F32),
            pltpu.VMEM((COEF, ROWS), F32),
            pltpu.VMEM((TABLES, COEF, COEF), BF16),
            pltpu.VMEM((COEF, WAVES), BF16),
            pltpu.VMEM((WAVES, COEF), BF16),
            pltpu.VMEM((COEF, WAVES), BF16),
            pltpu.VMEM((ROWS, WAVES), BF16),
            pltpu.VMEM((COEF, ROWS), F32),
            pltpu.VMEM((COEF, ROWS), F32),
            pltpu.VMEM((BLOCKS, 1, WAVES), F32),
            pltpu.VMEM((BLOCKS, 1, WAVES), F32),
            pltpu.VMEM((GROUP, 1, 128), F32),
            pltpu.VMEM((BLOCKS, 1, 128), F32),
            pltpu.VMEM((GROUP, 1, 128), F32),
            pltpu.VMEM((BLOCKS, 1, 128), F32),
            dma((5,)),
            dma((2,)),
            dma((SENDS,)),
            dma((GROUP, CHUNKS)),
            dma((SENDS,)),
            dma((GROUP, CHUNKS)),
            *blk_sems,
            *blk_sems,
            *grp_sems,
            *blk_sems,
            *grp_sems,
            *blk_sems,
        ],
        compiler_params=pltpu.CompilerParams(
            collective_id=0, has_side_effects=True, vmem_limit_bytes=56 * 2**20
        ),
    )(
        owner_dev[0, :, 0],
        near_row[0],
        table_id[0],
        u,
        mie_coef[0].T,
        tables,
        wave_out,
        wave_in.T,
        plane_angle[0],
        far_trans[0, 0],
    )
    y1, y2, rest_first = scal[0, 0], scal[0, 1], scal[0, 2]
    sol = y1 * u + y2 * (rest_first * u - b1)
    res = u - y1 * (u - b1) - y2 * (rest_first * (u - b1) - (b1 - q))
    return sol.T[None], res.T[None], hess.T


def solution(mesh):
    return jax.shard_map(
        body,
        mesh=mesh,
        in_specs=(
            P("blk", "grp", None),
            P("blk", "grp", None),
            P("blk", "grp", None),
            P("blk", "grp"),
            P("blk", "grp"),
            P(),
            P(),
            P(),
            P("blk", "grp", None),
            P("blk", "grp", None, None),
        ),
        out_specs=(P("blk", "grp", None), P("blk", "grp", None), P()),
        check_vma=False,
    )
```

```python
import functools

import jax
import jax.numpy as jnp
from jax import lax
from jax.experimental import pallas as pl
from jax.experimental.pallas import tpu as pltpu
from jax.sharding import PartitionSpec as P

MESH = pl.DeviceIdType.MESH
F32 = jnp.float32
BF16 = jnp.bfloat16

epsilon = 1e-06

ROWS = 1024
COEF = 240
WAVES = 512
TABLES = 8
PER_ROW = 3
GROUP = 16
BLOCKS = 8
TILE = 256
TILES = ROWS // TILE
UNROLL = 32

CHUNKS = 2 * TILES
CHUNK_ROWS = tuple((tile * TILE + half * 144, (144, 112)[half]) for tile in range(TILES) for half in range(2))
Z_FIRST = (True, False) * TILES
GO_RIGHT = (True, True, False, False) * (TILES // 2)


class Gather:
    def __init__(self, gbuf, send_sems, recv_sems):
        self.gbuf, self.send_sems, self.recv_sems = gbuf, send_sems, recv_sems
        g = lax.axis_index("grp")
        self.z, self.y, self.c = g // 8, (g // 2) % 4, g % 2
        self.me = g
        self.right = self.place(0, 1)
        self.left = self.place(0, 3)
        self.across = self.place(1, 0)
        self.partner = self.place(0, 0, 1)
        self.sent = []

    def place(self, dz, dy, dc=0):
        return ((self.z + dz) % 2) * 8 + ((self.y + dy) % 4) * 2 + (self.c + dc) % 2

    def copy(self, origin, chunk, device, slot):
        begin, count = CHUNK_ROWS[chunk]
        rows = pl.ds(origin * ROWS + begin, count)
        return pltpu.make_async_remote_copy(
            src_ref=self.gbuf.at[rows],
            dst_ref=self.gbuf.at[rows],
            send_sem=self.send_sems.at[slot],
            recv_sem=self.recv_sems.at[origin, chunk],
            device_id={"grp": device},
            device_id_type=MESH,
        )

    def send(self, origin, chunk, *devices):
        for device in devices:
            copy = self.copy(origin, chunk, device, len(self.sent))
            copy.start()
            self.sent.append(copy)

    def wait(self, origin, chunk):
        self.copy(origin, chunk, self.partner, 0).wait_recv()

    def store(self, tile, coded):
        start = pl.multiple_of(self.me * ROWS + tile * TILE, TILE)
        self.gbuf[pl.ds(start, TILE)] = coded.reshape(TILE, 2, 128)

    def start(self, tile):
        for k in (2 * tile, 2 * tile + 1):
            self.send(self.me, k, self.right, self.left, self.across, self.partner)

    def level_one(self):
        for k in range(CHUNKS):
            extra = () if Z_FIRST[k] else (self.across,)
            origin = self.place(0, 3)
            self.wait(origin, k)
            self.send(origin, k, *((self.right,) if GO_RIGHT[k] else ()), *extra, self.partner)
            origin = self.place(0, 1)
            self.wait(origin, k)
            self.send(origin, k, *(() if GO_RIGHT[k] else (self.left,)), *extra, self.partner)
            origin = self.place(1, 0)
            self.wait(origin, k)
            self.send(origin, k, *((self.right, self.left) if Z_FIRST[k] else ()), self.partner)

    def level_two(self):
        for k in range(CHUNKS):
            origin = self.place(0, 2)
            self.wait(origin, k)
            self.send(origin, k, *(() if Z_FIRST[k] else (self.across,)), self.partner)
            origin = self.place(1, 3)
            self.wait(origin, k)
            self.send(origin, k, *((self.right,) if Z_FIRST[k] and GO_RIGHT[k] else ()), self.partner)
            origin = self.place(1, 1)
            self.wait(origin, k)
            self.send(origin, k, *((self.left,) if Z_FIRST[k] and not GO_RIGHT[k] else ()), self.partner)

    def level_three(self):
        for k in range(CHUNKS):
            origin = self.place(1, 2)
            self.wait(origin, k)
            self.send(origin, k, self.partner)

    def finish(self):
        for dz in range(2):
            for dy in (0, 1, 3, 2):
                for k in range(CHUNKS):
                    self.wait(self.place(dz, dy, 1), k)

    def drain(self):
        for copy in self.sent:
            copy.wait_send()


SENDS = CHUNKS * 15


class Share:
    def __init__(self, buf, send_sems, recv_sems, axis, size):
        self.buf, self.send_sems, self.recv_sems, self.axis, self.size = buf, send_sems, recv_sems, axis, size
        self.slot = lax.axis_index(axis)

    def copy(self, source, target, step):
        return pltpu.make_async_remote_copy(
            src_ref=self.buf.at[source],
            dst_ref=self.buf.at[source],
            send_sem=self.send_sems.at[step - 1],
            recv_sem=self.recv_sems.at[source],
            device_id={self.axis: target},
            device_id_type=MESH,
        )

    def start(self, row):
        self.buf[pl.ds(self.slot, 1)] = row.reshape(1, 1, row.shape[1])
        for step in range(1, self.size):
            self.copy(self.slot, (self.slot + step) % self.size, step).start()

    def finish(self):
        for step in range(1, self.size):
            other = (self.slot + step) % self.size
            self.copy(other, other, step).wait_recv()
        for step in range(1, self.size):
            self.copy(self.slot, (self.slot + step) % self.size, step).wait_send()
        return self.buf[...].reshape(self.size, self.buf.shape[2])


def row_of(*values):
    lane = lax.broadcasted_iota(jnp.int32, (1, 128), 1)
    row = jnp.zeros((1, 128), F32)
    for place, value in enumerate(values):
        row = jnp.where(lane == place, value, row)
    return row


def column(rows, place):
    lane = lax.broadcasted_iota(jnp.int32, rows.shape, 1)
    return jnp.sum(jnp.where(lane == place, rows, 0.0), axis=1, keepdims=True)


def total(value):
    return jnp.sum(jnp.sum(value, axis=0, keepdims=True), axis=1, keepdims=True)


def spread_stats(rows):
    squares, inner, left, slope = (column(rows, place) for place in range(4))
    squares_all = jnp.sum(squares, axis=0, keepdims=True)
    inner_all = jnp.sum(inner, axis=0, keepdims=True)
    slope_all = inner_all / jnp.maximum(squares_all, 1e-30)
    gap = slope - slope_all
    left_all = jnp.sum(left + gap * gap * squares, axis=0, keepdims=True)
    return squares_all, inner_all, left_all, slope_all


def rows_of(tile):
    return pl.ds(pl.multiple_of(tile * TILE, TILE), TILE)


def cols_of(tile):
    return slice(tile * TILE, (tile + 1) * TILE)


def turned(tall):
    return jnp.concatenate([tall, jnp.zeros((256 - COEF, TILE), tall.dtype)], axis=0).T


def kernel(
    owners_hbm,
    near_rows_hbm,
    table_ids_hbm,
    u_hbm,
    mie_hbm,
    tables_hbm,
    wave_out_hbm,
    wave_in_hbm,
    angle_hbm,
    trans_hbm,
    b1_hbm,
    q_hbm,
    scal_ref,
    hess_ref,
    gbuf_a,
    gbuf_b,
    owners,
    near_rows,
    table_ids,
    u_ref,
    trans_ref,
    places,
    picked_a,
    picked_b,
    ids_wide,
    ids,
    padded,
    cosine,
    base,
    coded,
    mie,
    mie_tall,
    tables,
    wave_out,
    wave_in,
    wave_in_tall,
    angle,
    b1_tall,
    q_tall,
    wbuf_a,
    wbuf_b,
    stats_a,
    stats_b,
    stats_c,
    stats_d,
    u_sems,
    in_sems,
    out_sems,
    aga_send,
    aga_recv,
    agb_send,
    agb_recv,
    wa_send,
    wa_recv,
    wb_send,
    wb_recv,
    a_send,
    a_recv,
    b_send,
    b_recv,
    c_send,
    c_recv,
    d_send,
    d_recv,
):
    g = lax.axis_index("grp")
    b = lax.axis_index("blk")
    barrier = pltpu.get_barrier_semaphore()
    for step in range(1, GROUP):
        pl.semaphore_signal(barrier, inc=1, device_id={"grp": (g + step) % GROUP}, device_id_type=MESH)
    for step in range(1, BLOCKS):
        pl.semaphore_signal(barrier, inc=1, device_id={"blk": (b + step) % BLOCKS}, device_id_type=MESH)

    tall_loads = [
        pltpu.make_async_copy(u_hbm.at[:, cols_of(tile)], u_ref.at[:, cols_of(tile)], u_sems.at[tile])
        for tile in range(TILES)
    ]
    for load in tall_loads:
        load.start()
    loads = [
        pltpu.make_async_copy(source, target, in_sems.at[place])
        for place, (source, target) in enumerate(
            (
                (angle_hbm, angle),
                (wave_out_hbm, wave_out),
                (wave_in_hbm, wave_in_tall),
                (mie_hbm, mie_tall),
                (tables_hbm, tables),
                (trans_hbm, trans_ref),
                (owners_hbm, owners),
                (near_rows_hbm, near_rows),
                (table_ids_hbm, table_ids),
            )
        )
    ]
    for load in loads:
        load.start()

    first = Gather(gbuf_a, aga_send, aga_recv)
    second = Gather(gbuf_b, agb_send, agb_recv)
    waves_first = Share(wbuf_a, wa_send, wa_recv, "blk", BLOCKS)
    waves_second = Share(wbuf_b, wb_send, wb_recv, "blk", BLOCKS)
    share_a = Share(stats_a, a_send, a_recv, "grp", GROUP)
    share_b = Share(stats_b, b_send, b_recv, "blk", BLOCKS)
    share_c = Share(stats_c, c_send, c_recv, "grp", GROUP)
    share_d = Share(stats_d, d_send, d_recv, "blk", BLOCKS)

    for tile in range(TILES):
        tall_loads[tile].wait()
        block = turned(u_ref[:, cols_of(tile)]).astype(BF16)
        coded[rows_of(tile), :] = block
        first.store(tile, block)
        if tile == 0:
            pl.semaphore_wait(barrier, GROUP + BLOCKS - 2)
        first.start(tile)

    def tall_sums(step, count):
        sums = (jnp.zeros((1, 1), F32),) * count
        for tile in range(TILES):
            sums = step(cols_of(tile), sums)
        return sums

    def own_wave():
        def step(tile, wave):
            rows = rows_of(tile)
            outgoing = jnp.dot(coded[rows, 0:COEF], wave_out[...], preferred_element_type=F32)
            return wave + jnp.sum(cosine[rows, :] * outgoing, axis=0, keepdims=True)

        return lax.fori_loop(0, TILES, step, jnp.zeros((1, WAVES), F32))

    def far_field(waves):
        arrived = waves.finish()
        incoming = jnp.zeros((1, WAVES), F32)
        for c in range(BLOCKS):
            term = trans_ref[c : c + 1, :] * arrived[c : c + 1, :]
            incoming = incoming + jnp.where(b == c, jnp.zeros_like(term), term)

        @pl.loop(0, TILES)
        def _(tile):
            rows = rows_of(tile)
            spread = (cosine[rows, :] * incoming).astype(BF16)
            base[rows, :] = jnp.dot(spread, wave_in[...], preferred_element_type=F32)

    def fields(gbuf, use):
        buffers = (picked_a, picked_b)
        blocks = [(tile, k) for tile in range(TILES) for k in range(PER_ROW)]

        def fetch(place, turn):
            tile, k = blocks[place]
            begin = k * ROWS + tile * TILE + turn * UNROLL
            values = [gbuf[places[begin + step]].astype(F32) for step in range(UNROLL)]
            for step, value in enumerate(values):
                buffers[place % 2][pl.ds((turn * UNROLL + step) * 2, 2), :] = value

        for turn in range(TABLES):
            fetch(0, turn)
        near = jnp.zeros((TILE, COEF), F32)
        for place, (tile, k) in enumerate(blocks):
            low = buffers[place % 2][pl.ds(0, TILE, 2), :]
            high = buffers[place % 2][pl.ds(1, TILE, 2), :]
            wanted = jnp.concatenate([low, high], axis=1).astype(BF16)
            table = ids[pl.ds(k * ROWS + tile * TILE, TILE), :]
            table = jnp.concatenate([table, table], axis=1)
            term = jnp.zeros((TILE, COEF), F32)
            for t in range(TABLES):
                if place + 1 < len(blocks):
                    fetch(place + 1, t)
                chosen = jnp.where(table == jnp.asarray(t, BF16), wanted, jnp.zeros_like(wanted))
                term = term + jnp.dot(chosen, padded[t], preferred_element_type=F32)
            near = near + term.astype(BF16).astype(F32)
            if k == PER_ROW - 1:
                rows = rows_of(tile)
                use(tile, mie[rows, 0:COEF] * (near + base[rows, :]))
                near = jnp.zeros((TILE, COEF), F32)

    def widened(block):
        return jnp.concatenate([block, jnp.zeros((TILE, 256 - COEF), F32)], axis=1)

    loads[0].wait()

    @pl.loop(0, TILES)
    def _(tile):
        rows = rows_of(tile)
        cosine[rows, :] = jnp.cos(angle[rows, :].astype(F32))

    loads[1].wait()
    waves_first.start(own_wave())
    first.level_one()
    for load in loads[2:]:
        load.wait()
    wave_in[...] = jnp.concatenate(
        [wave_in_tall[...].astype(F32), jnp.zeros((256 - COEF, WAVES), F32)], axis=0
    ).T[:, 0:COEF].astype(BF16)
    far_field(waves_first)
    padded[...] = jnp.zeros_like(padded)
    for t in range(TABLES):
        padded[t, 0:COEF, :] = tables[t]
    for tile in range(TILES):
        mie[rows_of(tile), :] = turned(mie_tall[:, cols_of(tile)])
    for k in range(PER_ROW):

        @pl.loop(0, ROWS // UNROLL)
        def _(turn):
            for step in range(UNROLL):
                row = turn * UNROLL + step
                request = row * PER_ROW + k
                places[k * ROWS + row] = owners[request] * ROWS + near_rows[request]
                value = jnp.full((1, 128), table_ids[request], jnp.int32).astype(F32)
                ids_wide[pl.ds(k * ROWS + row, 1), :] = value

    ids[...] = ids_wide[...].astype(BF16)

    def square(cols, sums):
        u = u_ref[:, cols]
        return (sums[0] + total(u * u),)

    (squares,) = tall_sums(square, 1)
    first.level_two()
    first.level_three()
    first.finish()

    def use_first(tile, block):
        block = widened(block)
        narrow = block.astype(BF16)
        coded[rows_of(tile), :] = narrow
        second.store(tile, narrow)
        second.start(tile)
        b1_tall[:, cols_of(tile)] = block.T[0:COEF]

    fields(gbuf_a, use_first)

    b1_out = pltpu.make_async_copy(b1_tall, b1_hbm, out_sems.at[0])
    b1_out.start()
    waves_second.start(own_wave())

    def product(cols, sums):
        return (sums[0] + total(u_ref[:, cols] * b1_tall[:, cols]),)

    (inner,) = tall_sums(product, 1)
    slope = inner / jnp.maximum(squares, 1e-30)

    def left_over(cols, sums):
        rest = b1_tall[:, cols] - slope * u_ref[:, cols]
        return (sums[0] + total(rest * rest),)

    (left,) = tall_sums(left_over, 1)
    share_a.start(row_of(squares, inner, left, slope))
    second.level_one()
    share_b.start(row_of(*spread_stats(share_a.finish())))
    far_field(waves_second)
    second.level_two()
    squares, inner, left, slope = spread_stats(share_b.finish())
    beta_squared = squares + epsilon
    beta = jnp.sqrt(beta_squared)
    h11 = (squares - inner) / beta_squared
    rest_first = (inner + epsilon) / beta_squared
    gap = slope - rest_first
    h21 = jnp.sqrt((left + gap * gap * squares) / beta_squared + epsilon)
    scale = 1.0 / (beta * h21)
    second.level_three()
    first.drain()
    second.finish()

    sums = [jnp.zeros((1, 1), F32)] * 5

    def use_second(tile, block):
        q = widened(block).T[0:COEF]
        cols = cols_of(tile)
        q_tall[:, cols] = q
        u, b1 = u_ref[:, cols], b1_tall[:, cols]
        v = (rest_first * u - b1) * scale
        w = (rest_first * (u - b1) - (b1 - q)) * scale
        for place, pair in enumerate((u * w, v * w, w * w, u * v, v * v)):
            sums[place] = sums[place] + total(pair)

    fields(gbuf_b, use_second)

    share_c.start(row_of(*sums))
    q_out = pltpu.make_async_copy(q_tall, q_hbm, out_sems.at[1])
    q_out.start()
    share_d.start(jnp.sum(share_c.finish(), axis=0, keepdims=True))
    second.drain()
    parts = jnp.sum(share_d.finish(), axis=0, keepdims=True)
    uw, vw, ww, uv, vv = (column(parts, place) for place in range(5))
    h12 = uw / beta
    h22 = vw
    left = ww + h12 * h12 * (squares / beta_squared - 2.0) + h22 * h22 * (vv - 2.0) + 2.0 * h12 * h22 * (uv / beta)
    h32 = jnp.sqrt(jnp.maximum(left, 0.0) + epsilon)
    gram_aa = h11 * h11 + h21 * h21
    gram_ab = h11 * h12 + h21 * h22
    gram_bb = h12 * h12 + h22 * h22 + h32 * h32
    rhs_first = beta * h11
    rhs_second = beta * h12
    determinant = gram_aa * gram_bb - gram_ab * gram_ab
    y1 = (gram_bb * rhs_first - gram_ab * rhs_second) / determinant
    y2 = (gram_aa * rhs_second - gram_ab * rhs_first) / determinant
    scal_ref[...] = row_of(y1 / beta, y2 * scale, rest_first)
    at_row = lax.broadcasted_iota(jnp.int32, (2, 3), 1)
    at_col = lax.broadcasted_iota(jnp.int32, (2, 3), 0)
    left_col = jnp.where(at_row == 0, h11, jnp.where(at_row == 1, h21, jnp.zeros((2, 3), F32)))
    right_col = jnp.where(at_row == 0, h12, jnp.where(at_row == 1, h22, h32))
    hess_ref[...] = jnp.where(at_col == 0, left_col, right_col)
    b1_out.wait()
    q_out.wait()


def combine(scal_ref, hess_in_ref, u_ref, b1_ref, q_ref, sol_ref, res_ref, hess_ref):
    scal = scal_ref[...]
    y1, y2, rest_first = (column(scal, place) for place in range(3))
    u, b1 = u_ref[...], b1_ref[...]
    sol_ref[...] = y1 * u + y2 * (rest_first * u - b1)
    image = u - b1
    res_ref[...] = u - y1 * image - y2 * (rest_first * image - (b1 - q_ref[...]))
    hess_ref[...] = hess_in_ref[...]


def body(incident, mie_coef, owner_dev, near_row, table_id, tables, wave_out, wave_in, plane_angle, far_trans):
    vmem = pl.BlockSpec(memory_space=pltpu.VMEM)
    anywhere = pl.BlockSpec(memory_space=pl.ANY)
    dma = pltpu.SemaphoreType.DMA
    u = incident[0].T
    blk_sems = [dma((BLOCKS - 1,)), dma((BLOCKS,))]
    grp_sems = [dma((GROUP - 1,)), dma((GROUP,))]
    b1, q, scal, hess = pl.pallas_call(
        kernel,
        out_shape=(
            jax.ShapeDtypeStruct((COEF, ROWS), F32),
            jax.ShapeDtypeStruct((COEF, ROWS), F32),
            jax.ShapeDtypeStruct((1, 128), F32),
            jax.ShapeDtypeStruct((2, 3), F32),
        ),
        in_specs=[anywhere] * 10,
        out_specs=(anywhere, anywhere, vmem, vmem),
        scratch_shapes=[
            pltpu.VMEM((GROUP * ROWS, 2, 128), BF16),
            pltpu.VMEM((GROUP * ROWS, 2, 128), BF16),
            pltpu.SMEM((PER_ROW * ROWS,), jnp.int32),
            pltpu.SMEM((PER_ROW * ROWS,), jnp.int32),
            pltpu.SMEM((PER_ROW * ROWS,), jnp.int32),
            pltpu.VMEM((COEF, ROWS), F32),
            pltpu.VMEM((BLOCKS, WAVES), F32),
            pltpu.SMEM((PER_ROW * ROWS,), jnp.int32),
            pltpu.VMEM((TILE * 2, 128), F32),
            pltpu.VMEM((TILE * 2, 128), F32),
            pltpu.VMEM((PER_ROW * ROWS, 128), F32),
            pltpu.VMEM((PER_ROW * ROWS, 128), BF16),
            pltpu.VMEM((TABLES, 256, COEF), BF16),
            pltpu.VMEM((ROWS, WAVES), F32),
            pltpu.VMEM((ROWS, COEF), F32),
            pltpu.VMEM((ROWS, 256), BF16),
            pltpu.VMEM((ROWS, 256), F32),
            pltpu.VMEM((COEF, ROWS), F32),
            pltpu.VMEM((TABLES, COEF, COEF), BF16),
            pltpu.VMEM((COEF, WAVES), BF16),
            pltpu.VMEM((WAVES, COEF), BF16),
            pltpu.VMEM((COEF, WAVES), BF16),
            pltpu.VMEM((ROWS, WAVES), BF16),
            pltpu.VMEM((COEF, ROWS), F32),
            pltpu.VMEM((COEF, ROWS), F32),
            pltpu.VMEM((BLOCKS, 1, WAVES), F32),
            pltpu.VMEM((BLOCKS, 1, WAVES), F32),
            pltpu.VMEM((GROUP, 1, 128), F32),
            pltpu.VMEM((BLOCKS, 1, 128), F32),
            pltpu.VMEM((GROUP, 1, 128), F32),
            pltpu.VMEM((BLOCKS, 1, 128), F32),
            dma((TILES,)),
            dma((9,)),
            dma((2,)),
            dma((SENDS,)),
            dma((GROUP, CHUNKS)),
            dma((SENDS,)),
            dma((GROUP, CHUNKS)),
            *blk_sems,
            *blk_sems,
            *grp_sems,
            *blk_sems,
            *grp_sems,
            *blk_sems,
        ],
        compiler_params=pltpu.CompilerParams(
            collective_id=0, has_side_effects=True, vmem_limit_bytes=56 * 2**20
        ),
    )(
        owner_dev[0, :, 0],
        near_row[0],
        table_id[0],
        u,
        mie_coef[0].T,
        tables,
        wave_out,
        wave_in.T,
        plane_angle[0],
        far_trans[0, 0],
    )
    strip = pl.BlockSpec((COEF, TILE), lambda tile: (0, tile))
    whole_scal = pl.BlockSpec((1, 128), lambda tile: (0, 0))
    whole_hess = pl.BlockSpec((2, 3), lambda tile: (0, 0))
    sol, res, hess = pl.pallas_call(
        combine,
        grid=(TILES,),
        out_shape=(
            jax.ShapeDtypeStruct((COEF, ROWS), F32),
            jax.ShapeDtypeStruct((COEF, ROWS), F32),
            jax.ShapeDtypeStruct((2, 3), F32),
        ),
        in_specs=[whole_scal, whole_hess, strip, strip, strip],
        out_specs=(strip, strip, whole_hess),
    )(scal, hess, u, b1, q)
    return sol.T[None], res.T[None], hess.T


def solution(mesh):
    return jax.shard_map(
        body,
        mesh=mesh,
        in_specs=(
            P("blk", "grp", None),
            P("blk", "grp", None),
            P("blk", "grp", None),
            P("blk", "grp"),
            P("blk", "grp"),
            P(),
            P(),
            P(),
            P("blk", "grp", None),
            P("blk", "grp", None, None),
        ),
        out_specs=(P("blk", "grp", None), P("blk", "grp", None), P()),
        check_vma=False,
    )
```

```python
import functools

import jax
import jax.numpy as jnp
from jax import lax
from jax.experimental import pallas as pl
from jax.experimental.pallas import tpu as pltpu
from jax.sharding import PartitionSpec as P

MESH = pl.DeviceIdType.MESH
F32 = jnp.float32
BF16 = jnp.bfloat16

epsilon = 1e-06

ROWS = 1024
COEF = 240
WAVES = 512
TABLES = 8
PER_ROW = 3
GROUP = 16
BLOCKS = 8
TILE = 256
TILES = ROWS // TILE
UNROLL = 32

CHUNKS = 2 * TILES
CHUNK_ROWS = tuple((tile * TILE + half * 144, (144, 112)[half]) for tile in range(TILES) for half in range(2))
Z_FIRST = (True, False) * TILES
GO_RIGHT = (True, True, False, False) * (TILES // 2)


class Gather:
    def __init__(self, gbuf, send_sems, recv_sems):
        self.gbuf, self.send_sems, self.recv_sems = gbuf, send_sems, recv_sems
        g = lax.axis_index("grp")
        self.z, self.y, self.c = g // 8, (g // 2) % 4, g % 2
        self.me = g
        self.right = self.place(0, 1)
        self.left = self.place(0, 3)
        self.across = self.place(1, 0)
        self.partner = self.place(0, 0, 1)
        self.sent = []

    def place(self, dz, dy, dc=0):
        return ((self.z + dz) % 2) * 8 + ((self.y + dy) % 4) * 2 + (self.c + dc) % 2

    def copy(self, origin, chunk, device, slot):
        begin, count = CHUNK_ROWS[chunk]
        rows = pl.ds(origin * ROWS + begin, count)
        return pltpu.make_async_remote_copy(
            src_ref=self.gbuf.at[rows],
            dst_ref=self.gbuf.at[rows],
            send_sem=self.send_sems.at[slot],
            recv_sem=self.recv_sems.at[origin, chunk],
            device_id={"grp": device},
            device_id_type=MESH,
        )

    def send(self, origin, chunk, *devices):
        for device in devices:
            copy = self.copy(origin, chunk, device, len(self.sent))
            copy.start()
            self.sent.append(copy)

    def wait(self, origin, chunk):
        self.copy(origin, chunk, self.partner, 0).wait_recv()

    def store(self, tile, coded):
        start = pl.multiple_of(self.me * ROWS + tile * TILE, TILE)
        self.gbuf[pl.ds(start, TILE)] = coded.reshape(TILE, 2, 128)

    def start(self, tile):
        for k in (2 * tile, 2 * tile + 1):
            self.send(self.me, k, self.right, self.left, self.across, self.partner)

    def level_one(self):
        last_hops = []
        for k in range(CHUNKS):
            z_first, onward = Z_FIRST[k], self.right if GO_RIGHT[k] else self.left
            for dy, from_behind in ((3, GO_RIGHT[k]), (1, not GO_RIGHT[k])):
                origin = self.place(0, dy)
                self.wait(origin, k)
                if from_behind and z_first:
                    last_hops.append((origin, k, onward))
                elif from_behind:
                    self.send(origin, k, onward)
                self.send(origin, k, *(() if z_first else (self.across,)), self.partner)
            origin = self.place(1, 0)
            self.wait(origin, k)
            if z_first:
                self.send(origin, k, onward)
                last_hops.append((origin, k, self.left if GO_RIGHT[k] else self.right))
            self.send(origin, k, self.partner)
        for origin, k, device in last_hops:
            self.send(origin, k, device)

    def level_two(self):
        self.ending = ending = []
        for k in range(CHUNKS):
            z_first, right = Z_FIRST[k], GO_RIGHT[k]
            if z_first:
                origin = self.place(1, 3 if right else 1)
                ending += [(self.place(1, 1 if right else 3), k), (self.place(0, 2), k)]
            else:
                origin = self.place(0, 2)
                ending += [(self.place(1, 3), k), (self.place(1, 1), k)]
            self.wait(origin, k)
            self.send(origin, k, (self.right if right else self.left) if z_first else self.across, self.partner)
    def level_three(self):
        for origin, k in self.ending:
            self.wait(origin, k)
            self.send(origin, k, self.partner)
        for k in range(CHUNKS):
            origin = self.place(1, 2)
            self.wait(origin, k)
            self.send(origin, k, self.partner)

    def finish(self):
        for dz in range(2):
            for dy in (0, 1, 3, 2):
                for k in range(CHUNKS):
                    self.wait(self.place(dz, dy, 1), k)

    def drain(self):
        for copy in self.sent:
            copy.wait_send()


SENDS = CHUNKS * 15


class Share:
    def __init__(self, buf, send_sems, recv_sems, axis, size):
        self.buf, self.send_sems, self.recv_sems, self.axis, self.size = buf, send_sems, recv_sems, axis, size
        self.slot = lax.axis_index(axis)

    def copy(self, source, target, step):
        return pltpu.make_async_remote_copy(
            src_ref=self.buf.at[source],
            dst_ref=self.buf.at[source],
            send_sem=self.send_sems.at[step - 1],
            recv_sem=self.recv_sems.at[source],
            device_id={self.axis: target},
            device_id_type=MESH,
        )

    def start(self, row):
        self.buf[pl.ds(self.slot, 1)] = row.reshape(1, 1, row.shape[1])
        for step in range(1, self.size):
            self.copy(self.slot, (self.slot + step) % self.size, step).start()

    def finish(self):
        for step in range(1, self.size):
            other = (self.slot + step) % self.size
            self.copy(other, other, step).wait_recv()
        for step in range(1, self.size):
            self.copy(self.slot, (self.slot + step) % self.size, step).wait_send()
        return self.buf[...].reshape(self.size, self.buf.shape[2])


def row_of(*values):
    lane = lax.broadcasted_iota(jnp.int32, (1, 128), 1)
    row = jnp.zeros((1, 128), F32)
    for place, value in enumerate(values):
        row = jnp.where(lane == place, value, row)
    return row


def column(rows, place):
    lane = lax.broadcasted_iota(jnp.int32, rows.shape, 1)
    return jnp.sum(jnp.where(lane == place, rows, 0.0), axis=1, keepdims=True)


def total(value):
    return jnp.sum(jnp.sum(value, axis=0, keepdims=True), axis=1, keepdims=True)


def spread_stats(rows):
    squares, inner, left, slope = (column(rows, place) for place in range(4))
    squares_all = jnp.sum(squares, axis=0, keepdims=True)
    inner_all = jnp.sum(inner, axis=0, keepdims=True)
    slope_all = inner_all / jnp.maximum(squares_all, 1e-30)
    gap = slope - slope_all
    left_all = jnp.sum(left + gap * gap * squares, axis=0, keepdims=True)
    return squares_all, inner_all, left_all, slope_all


def rows_of(tile):
    return pl.ds(pl.multiple_of(tile * TILE, TILE), TILE)


def cols_of(tile):
    return slice(tile * TILE, (tile + 1) * TILE)


def turned(tall):
    return jnp.concatenate([tall, jnp.zeros((256 - COEF, TILE), tall.dtype)], axis=0).T


def kernel(
    owners_hbm,
    near_rows_hbm,
    table_ids_hbm,
    u_hbm,
    mie_hbm,
    tables_hbm,
    wave_out_hbm,
    wave_in_hbm,
    angle_hbm,
    trans_hbm,
    b1_hbm,
    q_hbm,
    scal_ref,
    hess_ref,
    gbuf_a,
    gbuf_b,
    owners,
    near_rows,
    table_ids,
    u_ref,
    trans_ref,
    places,
    picked_a,
    picked_b,
    ids_wide,
    masks,
    padded,
    cosine,
    base,
    coded,
    mie,
    mie_tall,
    tables,
    wave_out,
    wave_in,
    wave_in_tall,
    angle,
    b1_tall,
    q_tall,
    wbuf_a,
    wbuf_b,
    stats_a,
    stats_b,
    stats_c,
    stats_d,
    places_sem,
    u_sems,
    in_sems,
    out_sems,
    aga_send,
    aga_recv,
    agb_send,
    agb_recv,
    wa_send,
    wa_recv,
    wb_send,
    wb_recv,
    a_send,
    a_recv,
    b_send,
    b_recv,
    c_send,
    c_recv,
    d_send,
    d_recv,
):
    g = lax.axis_index("grp")
    b = lax.axis_index("blk")
    barrier = pltpu.get_barrier_semaphore()
    for step in range(1, GROUP):
        pl.semaphore_signal(barrier, inc=1, device_id={"grp": (g + step) % GROUP}, device_id_type=MESH)
    for step in range(1, BLOCKS):
        pl.semaphore_signal(barrier, inc=1, device_id={"blk": (b + step) % BLOCKS}, device_id_type=MESH)

    tall_loads = [
        pltpu.make_async_copy(u_hbm.at[:, cols_of(tile)], u_ref.at[:, cols_of(tile)], u_sems.at[tile])
        for tile in range(TILES)
    ]
    for load in tall_loads:
        load.start()
    loads = [
        pltpu.make_async_copy(source, target, in_sems.at[place])
        for place, (source, target) in enumerate(
            (
                (angle_hbm, angle),
                (wave_out_hbm, wave_out),
                (wave_in_hbm, wave_in_tall),
                (mie_hbm, mie_tall),
                (tables_hbm, tables),
                (trans_hbm, trans_ref),
                (owners_hbm, owners),
                (near_rows_hbm, near_rows),
                (table_ids_hbm, table_ids),
            )
        )
    ]
    for load in loads:
        load.start()

    first = Gather(gbuf_a, aga_send, aga_recv)
    second = Gather(gbuf_b, agb_send, agb_recv)
    waves_first = Share(wbuf_a, wa_send, wa_recv, "blk", BLOCKS)
    waves_second = Share(wbuf_b, wb_send, wb_recv, "blk", BLOCKS)
    share_a = Share(stats_a, a_send, a_recv, "grp", GROUP)
    share_b = Share(stats_b, b_send, b_recv, "blk", BLOCKS)
    share_c = Share(stats_c, c_send, c_recv, "grp", GROUP)
    share_d = Share(stats_d, d_send, d_recv, "blk", BLOCKS)

    for tile in range(TILES):
        tall_loads[tile].wait()
        block = turned(u_ref[:, cols_of(tile)]).astype(BF16)
        coded[rows_of(tile), :] = block
        first.store(tile, block)
        if tile == 0:
            pl.semaphore_wait(barrier, GROUP + BLOCKS - 2)
        first.start(tile)

    def tall_sums(step, count):
        sums = (jnp.zeros((1, 1), F32),) * count
        for tile in range(TILES):
            sums = step(cols_of(tile), sums)
        return sums

    def own_wave():
        def step(tile, wave):
            rows = rows_of(tile)
            outgoing = jnp.dot(coded[rows, 0:COEF], wave_out[...], preferred_element_type=F32)
            return wave + jnp.sum(cosine[rows, :] * outgoing, axis=0, keepdims=True)

        return lax.fori_loop(0, TILES, step, jnp.zeros((1, WAVES), F32))

    def far_field(waves):
        arrived = waves.finish()
        incoming = jnp.zeros((1, WAVES), F32)
        for c in range(BLOCKS):
            term = trans_ref[c : c + 1, :] * arrived[c : c + 1, :]
            incoming = incoming + jnp.where(b == c, jnp.zeros_like(term), term)

        @pl.loop(0, TILES)
        def _(tile):
            rows = rows_of(tile)
            spread = (cosine[rows, :] * incoming).astype(BF16)
            base[rows, :] = jnp.dot(spread, wave_in[...], preferred_element_type=F32)

    def fields(gbuf, use):
        buffers = (picked_a, picked_b)
        blocks = [(tile, k) for tile in range(TILES) for k in range(PER_ROW)]

        def fetch(place, turn):
            tile, k = blocks[place]
            begin = tile * TILE + turn * UNROLL
            values = [gbuf[places[(begin + step) * PER_ROW + k]].astype(F32) for step in range(UNROLL)]
            for step, value in enumerate(values):
                buffers[place % 2][pl.ds((turn * UNROLL + step) * 2, 2), :] = value

        for turn in range(TABLES):
            fetch(0, turn)
        near = jnp.zeros((TILE, COEF), F32)
        for place, (tile, k) in enumerate(blocks):
            low = buffers[place % 2][pl.ds(0, TILE, 2), :]
            high = buffers[place % 2][pl.ds(1, TILE, 2), :]
            wanted = jnp.concatenate([low, high], axis=1).astype(BF16)
            rows = pl.ds(k * ROWS + tile * TILE, TILE)
            chosen = []
            for t in range(TABLES):
                if place + 1 < len(blocks):
                    fetch(place + 1, t)
                mask = masks[t, rows, :]
                chosen.append(wanted * jnp.concatenate([mask, mask], axis=1))
            term = jnp.dot(jnp.concatenate(chosen, axis=1), padded[...], preferred_element_type=F32)
            near = near + term.astype(BF16).astype(F32)
            if k == PER_ROW - 1:
                rows = rows_of(tile)
                use(tile, mie[rows, 0:COEF] * (near + base[rows, :]))
                near = jnp.zeros((TILE, COEF), F32)

    def widened(block):
        return jnp.concatenate([block, jnp.zeros((TILE, 256 - COEF), F32)], axis=1)

    loads[0].wait()

    @pl.loop(0, TILES)
    def _(tile):
        rows = rows_of(tile)
        cosine[rows, :] = jnp.cos(angle[rows, :].astype(F32))

    loads[1].wait()
    waves_first.start(own_wave())
    first.level_one()
    for load in loads[2:]:
        load.wait()
    owners[...] = owners[...] * ROWS + near_rows[...]
    to_places = pltpu.make_async_copy(owners, places, places_sem)
    to_places.start()
    wave_in[...] = jnp.concatenate(
        [wave_in_tall[...].astype(F32), jnp.zeros((256 - COEF, WAVES), F32)], axis=0
    ).T[:, 0:COEF].astype(BF16)
    far_field(waves_first)
    first.level_two()
    padded[...] = jnp.zeros_like(padded)
    for t in range(TABLES):
        padded[t * 256 : t * 256 + COEF, :] = tables[t]
    for tile in range(TILES):
        mie[rows_of(tile), :] = turned(mie_tall[:, cols_of(tile)])
    for k in range(PER_ROW):

        @pl.loop(0, ROWS // UNROLL)
        def _(turn):
            for step in range(UNROLL):
                row = turn * UNROLL + step
                request = row * PER_ROW + k
                value = jnp.full((1, 128), table_ids[request], jnp.int32).astype(F32)
                ids_wide[pl.ds(k * ROWS + row, 1), :] = value

    @pl.loop(0, PER_ROW * TILES)
    def _(part):
        rows = rows_of(part)
        table = ids_wide[rows, :]
        for t in range(TABLES):
            masks[t, rows, :] = jnp.where(table == float(t), 1.0, 0.0).astype(BF16)

    def square(cols, sums):
        u = u_ref[:, cols]
        return (sums[0] + total(u * u),)

    (squares,) = tall_sums(square, 1)
    to_places.wait()
    first.level_three()
    first.finish()

    def use_first(tile, block):
        block = widened(block)
        narrow = block.astype(BF16)
        coded[rows_of(tile), :] = narrow
        second.store(tile, narrow)
        second.start(tile)
        b1_tall[:, cols_of(tile)] = block.T[0:COEF]

    fields(gbuf_a, use_first)

    b1_out = pltpu.make_async_copy(b1_tall, b1_hbm, out_sems.at[0])
    b1_out.start()
    waves_second.start(own_wave())

    def product(cols, sums):
        return (sums[0] + total(u_ref[:, cols] * b1_tall[:, cols]),)

    (inner,) = tall_sums(product, 1)
    slope = inner / jnp.maximum(squares, 1e-30)

    def left_over(cols, sums):
        rest = b1_tall[:, cols] - slope * u_ref[:, cols]
        return (sums[0] + total(rest * rest),)

    (left,) = tall_sums(left_over, 1)
    share_a.start(row_of(squares, inner, left, slope))
    second.level_one()
    share_b.start(row_of(*spread_stats(share_a.finish())))
    far_field(waves_second)
    second.level_two()
    squares, inner, left, slope = spread_stats(share_b.finish())
    beta_squared = squares + epsilon
    beta = jnp.sqrt(beta_squared)
    h11 = (squares - inner) / beta_squared
    rest_first = (inner + epsilon) / beta_squared
    gap = slope - rest_first
    h21 = jnp.sqrt((left + gap * gap * squares) / beta_squared + epsilon)
    scale = 1.0 / (beta * h21)
    second.level_three()
    first.drain()
    second.finish()

    sums = [jnp.zeros((1, 1), F32)] * 5

    def use_second(tile, block):
        q = widened(block).T[0:COEF]
        cols = cols_of(tile)
        q_tall[:, cols] = q
        u, b1 = u_ref[:, cols], b1_tall[:, cols]
        v = (rest_first * u - b1) * scale
        w = (rest_first * (u - b1) - (b1 - q)) * scale
        for place, pair in enumerate((u * w, v * w, w * w, u * v, v * v)):
            sums[place] = sums[place] + total(pair)

    fields(gbuf_b, use_second)

    share_c.start(row_of(*sums))
    q_out = pltpu.make_async_copy(q_tall, q_hbm, out_sems.at[1])
    q_out.start()
    share_d.start(jnp.sum(share_c.finish(), axis=0, keepdims=True))
    second.drain()
    parts = jnp.sum(share_d.finish(), axis=0, keepdims=True)
    uw, vw, ww, uv, vv = (column(parts, place) for place in range(5))
    h12 = uw / beta
    h22 = vw
    left = ww + h12 * h12 * (squares / beta_squared - 2.0) + h22 * h22 * (vv - 2.0) + 2.0 * h12 * h22 * (uv / beta)
    h32 = jnp.sqrt(jnp.maximum(left, 0.0) + epsilon)
    gram_aa = h11 * h11 + h21 * h21
    gram_ab = h11 * h12 + h21 * h22
    gram_bb = h12 * h12 + h22 * h22 + h32 * h32
    rhs_first = beta * h11
    rhs_second = beta * h12
    determinant = gram_aa * gram_bb - gram_ab * gram_ab
    y1 = (gram_bb * rhs_first - gram_ab * rhs_second) / determinant
    y2 = (gram_aa * rhs_second - gram_ab * rhs_first) / determinant
    scal_ref[...] = row_of(y1 / beta, y2 * scale, rest_first)
    at_row = lax.broadcasted_iota(jnp.int32, (2, 3), 1)
    at_col = lax.broadcasted_iota(jnp.int32, (2, 3), 0)
    left_col = jnp.where(at_row == 0, h11, jnp.where(at_row == 1, h21, jnp.zeros((2, 3), F32)))
    right_col = jnp.where(at_row == 0, h12, jnp.where(at_row == 1, h22, h32))
    hess_ref[...] = jnp.where(at_col == 0, left_col, right_col)
    b1_out.wait()
    q_out.wait()


def combine(scal_ref, hess_in_ref, u_ref, b1_ref, q_ref, sol_ref, res_ref, hess_ref):
    scal = scal_ref[...]
    y1, y2, rest_first = (column(scal, place) for place in range(3))
    u, b1 = u_ref[...], b1_ref[...]
    sol_ref[...] = y1 * u + y2 * (rest_first * u - b1)
    image = u - b1
    res_ref[...] = u - y1 * image - y2 * (rest_first * image - (b1 - q_ref[...]))
    hess_ref[...] = hess_in_ref[...]


def body(incident, mie_coef, owner_dev, near_row, table_id, tables, wave_out, wave_in, plane_angle, far_trans):
    vmem = pl.BlockSpec(memory_space=pltpu.VMEM)
    anywhere = pl.BlockSpec(memory_space=pl.ANY)
    dma = pltpu.SemaphoreType.DMA
    u = incident[0].T
    blk_sems = [dma((BLOCKS - 1,)), dma((BLOCKS,))]
    grp_sems = [dma((GROUP - 1,)), dma((GROUP,))]
    b1, q, scal, hess = pl.pallas_call(
        kernel,
        out_shape=(
            jax.ShapeDtypeStruct((COEF, ROWS), F32),
            jax.ShapeDtypeStruct((COEF, ROWS), F32),
            jax.ShapeDtypeStruct((1, 128), F32),
            jax.ShapeDtypeStruct((2, 3), F32),
        ),
        in_specs=[anywhere] * 10,
        out_specs=(anywhere, anywhere, vmem, vmem),
        scratch_shapes=[
            pltpu.VMEM((GROUP * ROWS, 2, 128), BF16),
            pltpu.VMEM((GROUP * ROWS, 2, 128), BF16),
            pltpu.VMEM((PER_ROW * ROWS,), jnp.int32),
            pltpu.VMEM((PER_ROW * ROWS,), jnp.int32),
            pltpu.SMEM((PER_ROW * ROWS,), jnp.int32),
            pltpu.VMEM((COEF, ROWS), F32),
            pltpu.VMEM((BLOCKS, WAVES), F32),
            pltpu.SMEM((PER_ROW * ROWS,), jnp.int32),
            pltpu.VMEM((TILE * 2, 128), F32),
            pltpu.VMEM((TILE * 2, 128), F32),
            pltpu.VMEM((PER_ROW * ROWS, 128), F32),
            pltpu.VMEM((TABLES, PER_ROW * ROWS, 128), BF16),
            pltpu.VMEM((TABLES * 256, COEF), BF16),
            pltpu.VMEM((ROWS, WAVES), F32),
            pltpu.VMEM((ROWS, COEF), F32),
            pltpu.VMEM((ROWS, 256), BF16),
            pltpu.VMEM((ROWS, 256), F32),
            pltpu.VMEM((COEF, ROWS), F32),
            pltpu.VMEM((TABLES, COEF, COEF), BF16),
            pltpu.VMEM((COEF, WAVES), BF16),
            pltpu.VMEM((WAVES, COEF), BF16),
            pltpu.VMEM((COEF, WAVES), BF16),
            pltpu.VMEM((ROWS, WAVES), BF16),
            pltpu.VMEM((COEF, ROWS), F32),
            pltpu.VMEM((COEF, ROWS), F32),
            pltpu.VMEM((BLOCKS, 1, WAVES), F32),
            pltpu.VMEM((BLOCKS, 1, WAVES), F32),
            pltpu.VMEM((GROUP, 1, 128), F32),
            pltpu.VMEM((BLOCKS, 1, 128), F32),
            pltpu.VMEM((GROUP, 1, 128), F32),
            pltpu.VMEM((BLOCKS, 1, 128), F32),
            dma,
            dma((TILES,)),
            dma((9,)),
            dma((2,)),
            dma((SENDS,)),
            dma((GROUP, CHUNKS)),
            dma((SENDS,)),
            dma((GROUP, CHUNKS)),
            *blk_sems,
            *blk_sems,
            *grp_sems,
            *blk_sems,
            *grp_sems,
            *blk_sems,
        ],
        compiler_params=pltpu.CompilerParams(
            collective_id=0, has_side_effects=True, vmem_limit_bytes=56 * 2**20
        ),
    )(
        owner_dev[0, :, 0],
        near_row[0],
        table_id[0],
        u,
        mie_coef[0].T,
        tables,
        wave_out,
        wave_in.T,
        plane_angle[0],
        far_trans[0, 0],
    )
    strip = pl.BlockSpec((COEF, TILE), lambda tile: (0, tile))
    whole_scal = pl.BlockSpec((1, 128), lambda tile: (0, 0))
    whole_hess = pl.BlockSpec((2, 3), lambda tile: (0, 0))
    sol, res, hess = pl.pallas_call(
        combine,
        grid=(TILES,),
        out_shape=(
            jax.ShapeDtypeStruct((COEF, ROWS), F32),
            jax.ShapeDtypeStruct((COEF, ROWS), F32),
            jax.ShapeDtypeStruct((2, 3), F32),
        ),
        in_specs=[whole_scal, whole_hess, strip, strip, strip],
        out_specs=(strip, strip, whole_hess),
    )(scal, hess, u, b1, q)
    return sol.T[None], res.T[None], hess.T


def solution(mesh):
    return jax.shard_map(
        body,
        mesh=mesh,
        in_specs=(
            P("blk", "grp", None),
            P("blk", "grp", None),
            P("blk", "grp", None),
            P("blk", "grp"),
            P("blk", "grp"),
            P(),
            P(),
            P(),
            P("blk", "grp", None),
            P("blk", "grp", None, None),
        ),
        out_specs=(P("blk", "grp", None), P("blk", "grp", None), P()),
        check_vma=False,
    )
```

```python
import functools

import jax
import jax.numpy as jnp
from jax import lax
from jax.experimental import pallas as pl
from jax.experimental.pallas import tpu as pltpu
from jax.sharding import PartitionSpec as P

MESH = pl.DeviceIdType.MESH
F32 = jnp.float32
BF16 = jnp.bfloat16

epsilon = 1e-06

ROWS = 1024
COEF = 240
WAVES = 512
TABLES = 8
PER_ROW = 3
GROUP = 16
BLOCKS = 8
TILE = 256
TILES = ROWS // TILE
UNROLL = 32

CHUNKS = 2 * TILES
CHUNK_ROWS = tuple((tile * TILE + half * 144, (144, 112)[half]) for tile in range(TILES) for half in range(2))
Z_FIRST = (True, False) * TILES
GO_RIGHT = (True, True, False, False) * (TILES // 2)


class Gather:
    def __init__(self, gbuf, send_sems, recv_sems):
        self.gbuf, self.send_sems, self.recv_sems = gbuf, send_sems, recv_sems
        g = lax.axis_index("grp")
        self.z, self.y, self.c = g // 8, (g // 2) % 4, g % 2
        self.me = g
        self.right = self.place(0, 1)
        self.left = self.place(0, 3)
        self.across = self.place(1, 0)
        self.partner = self.place(0, 0, 1)
        self.sent = []

    def place(self, dz, dy, dc=0):
        return ((self.z + dz) % 2) * 8 + ((self.y + dy) % 4) * 2 + (self.c + dc) % 2

    def copy(self, origin, chunk, device, slot):
        begin, count = CHUNK_ROWS[chunk]
        rows = pl.ds(origin * ROWS + begin, count)
        return pltpu.make_async_remote_copy(
            src_ref=self.gbuf.at[rows],
            dst_ref=self.gbuf.at[rows],
            send_sem=self.send_sems.at[slot],
            recv_sem=self.recv_sems.at[origin, chunk],
            device_id={"grp": device},
            device_id_type=MESH,
        )

    def send(self, origin, chunk, *devices):
        for device in devices:
            copy = self.copy(origin, chunk, device, len(self.sent))
            copy.start()
            self.sent.append(copy)

    def wait(self, origin, chunk):
        self.copy(origin, chunk, self.partner, 0).wait_recv()

    def store(self, tile, coded):
        start = pl.multiple_of(self.me * ROWS + tile * TILE, TILE)
        self.gbuf[pl.ds(start, TILE)] = coded.reshape(TILE, 2, 128)

    def start(self, tile):
        for k in (2 * tile, 2 * tile + 1):
            self.send(self.me, k, self.right, self.left, self.across, self.partner)

    def level_one(self):
        last_hops = []
        for k in range(CHUNKS):
            z_first, onward = Z_FIRST[k], self.right if GO_RIGHT[k] else self.left
            for dy, from_behind in ((3, GO_RIGHT[k]), (1, not GO_RIGHT[k])):
                origin = self.place(0, dy)
                self.wait(origin, k)
                if from_behind and z_first:
                    last_hops.append((origin, k, onward))
                elif from_behind:
                    self.send(origin, k, onward)
                self.send(origin, k, *(() if z_first else (self.across,)), self.partner)
            origin = self.place(1, 0)
            self.wait(origin, k)
            if z_first:
                self.send(origin, k, onward)
                last_hops.append((origin, k, self.left if GO_RIGHT[k] else self.right))
            self.send(origin, k, self.partner)
        for origin, k, device in last_hops:
            self.send(origin, k, device)

    def level_two(self):
        self.ending = ending = []
        for k in range(CHUNKS):
            z_first, right = Z_FIRST[k], GO_RIGHT[k]
            if z_first:
                origin = self.place(1, 3 if right else 1)
                ending += [(self.place(1, 1 if right else 3), k), (self.place(0, 2), k)]
            else:
                origin = self.place(0, 2)
                ending += [(self.place(1, 3), k), (self.place(1, 1), k)]
            self.wait(origin, k)
            self.send(origin, k, (self.right if right else self.left) if z_first else self.across, self.partner)
    def level_three(self):
        for origin, k in self.ending:
            self.wait(origin, k)
            self.send(origin, k, self.partner)
        for k in range(CHUNKS):
            origin = self.place(1, 2)
            self.wait(origin, k)
            self.send(origin, k, self.partner)

    def finish(self):
        for dz in range(2):
            for dy in (0, 1, 3, 2):
                for k in range(CHUNKS):
                    self.wait(self.place(dz, dy, 1), k)

    def drain(self):
        for copy in self.sent:
            copy.wait_send()


SENDS = CHUNKS * 15


class Share:
    def __init__(self, buf, send_sems, recv_sems, axis, size):
        self.buf, self.send_sems, self.recv_sems, self.axis, self.size = buf, send_sems, recv_sems, axis, size
        self.slot = lax.axis_index(axis)

    def copy(self, source, target, step):
        return pltpu.make_async_remote_copy(
            src_ref=self.buf.at[source],
            dst_ref=self.buf.at[source],
            send_sem=self.send_sems.at[step - 1],
            recv_sem=self.recv_sems.at[source],
            device_id={self.axis: target},
            device_id_type=MESH,
        )

    def start(self, row):
        self.buf[pl.ds(self.slot, 1)] = row.reshape(1, 1, row.shape[1])
        for step in range(1, self.size):
            self.copy(self.slot, (self.slot + step) % self.size, step).start()

    def finish(self):
        for step in range(1, self.size):
            other = (self.slot + step) % self.size
            self.copy(other, other, step).wait_recv()
        return self.buf[...].reshape(self.size, self.buf.shape[2])

    def drain(self):
        for step in range(1, self.size):
            self.copy(self.slot, (self.slot + step) % self.size, step).wait_send()


def row_of(*values):
    lane = lax.broadcasted_iota(jnp.int32, (1, 128), 1)
    row = jnp.zeros((1, 128), F32)
    for place, value in enumerate(values):
        row = jnp.where(lane == place, value, row)
    return row


def column(rows, place):
    lane = lax.broadcasted_iota(jnp.int32, rows.shape, 1)
    return jnp.sum(jnp.where(lane == place, rows, 0.0), axis=1, keepdims=True)


def total(value):
    return jnp.sum(jnp.sum(value, axis=0, keepdims=True), axis=1, keepdims=True)


def spread_stats(rows):
    squares, inner, left, slope = (column(rows, place) for place in range(4))
    squares_all = jnp.sum(squares, axis=0, keepdims=True)
    inner_all = jnp.sum(inner, axis=0, keepdims=True)
    slope_all = inner_all / jnp.maximum(squares_all, 1e-30)
    gap = slope - slope_all
    left_all = jnp.sum(left + gap * gap * squares, axis=0, keepdims=True)
    return squares_all, inner_all, left_all, slope_all


def rows_of(tile):
    return pl.ds(pl.multiple_of(tile * TILE, TILE), TILE)


def cols_of(tile):
    return slice(tile * TILE, (tile + 1) * TILE)


def turned(tall):
    return jnp.concatenate([tall, jnp.zeros((256 - COEF, TILE), tall.dtype)], axis=0).T


def kernel(
    owners_hbm,
    near_rows_hbm,
    table_ids_hbm,
    u_hbm,
    mie_hbm,
    tables_hbm,
    wave_out_hbm,
    wave_in_hbm,
    angle_hbm,
    trans_hbm,
    b1_hbm,
    q_hbm,
    scal_ref,
    hess_ref,
    gbuf_a,
    gbuf_b,
    owners,
    near_rows,
    table_ids,
    u_ref,
    trans_ref,
    places,
    picked_a,
    picked_b,
    ids_wide,
    masks,
    padded,
    cosine,
    base,
    coded,
    mie,
    mie_tall,
    tables,
    wave_out,
    wave_in,
    wave_in_tall,
    angle,
    b1_tall,
    q_tall,
    wbuf_a,
    wbuf_b,
    stats_a,
    stats_b,
    stats_c,
    stats_d,
    places_sem,
    u_sems,
    in_sems,
    out_sems,
    aga_send,
    aga_recv,
    agb_send,
    agb_recv,
    wa_send,
    wa_recv,
    wb_send,
    wb_recv,
    a_send,
    a_recv,
    b_send,
    b_recv,
    c_send,
    c_recv,
    d_send,
    d_recv,
):
    g = lax.axis_index("grp")
    b = lax.axis_index("blk")
    barrier = pltpu.get_barrier_semaphore()
    for step in range(1, GROUP):
        pl.semaphore_signal(barrier, inc=1, device_id={"grp": (g + step) % GROUP}, device_id_type=MESH)
    for step in range(1, BLOCKS):
        pl.semaphore_signal(barrier, inc=1, device_id={"blk": (b + step) % BLOCKS}, device_id_type=MESH)

    tall_loads = [
        pltpu.make_async_copy(u_hbm.at[:, cols_of(tile)], u_ref.at[:, cols_of(tile)], u_sems.at[tile])
        for tile in range(TILES)
    ]
    for load in tall_loads:
        load.start()
    loads = [
        pltpu.make_async_copy(source, target, in_sems.at[place])
        for place, (source, target) in enumerate(
            (
                (angle_hbm, angle),
                (wave_out_hbm, wave_out),
                (wave_in_hbm, wave_in_tall),
                (mie_hbm, mie_tall),
                (tables_hbm, tables),
                (trans_hbm, trans_ref),
                (owners_hbm, owners),
                (near_rows_hbm, near_rows),
                (table_ids_hbm, table_ids),
            )
        )
    ]
    for load in loads:
        load.start()

    first = Gather(gbuf_a, aga_send, aga_recv)
    second = Gather(gbuf_b, agb_send, agb_recv)
    waves_first = Share(wbuf_a, wa_send, wa_recv, "blk", BLOCKS)
    waves_second = Share(wbuf_b, wb_send, wb_recv, "blk", BLOCKS)
    share_a = Share(stats_a, a_send, a_recv, "grp", GROUP)
    share_b = Share(stats_b, b_send, b_recv, "blk", BLOCKS)
    share_c = Share(stats_c, c_send, c_recv, "grp", GROUP)
    share_d = Share(stats_d, d_send, d_recv, "blk", BLOCKS)

    for tile in range(TILES):
        tall_loads[tile].wait()
        block = turned(u_ref[:, cols_of(tile)]).astype(BF16)
        coded[rows_of(tile), :] = block
        first.store(tile, block)
        if tile == 0:
            pl.semaphore_wait(barrier, GROUP + BLOCKS - 2)
        first.start(tile)

    def tall_sums(step, count):
        sums = (jnp.zeros((1, 1), F32),) * count
        for tile in range(TILES):
            sums = step(cols_of(tile), sums)
        return sums

    def own_wave():
        def step(tile, wave):
            rows = rows_of(tile)
            outgoing = jnp.dot(coded[rows, 0:COEF], wave_out[...], preferred_element_type=F32)
            return wave + jnp.sum(cosine[rows, :] * outgoing, axis=0, keepdims=True)

        return lax.fori_loop(0, TILES, step, jnp.zeros((1, WAVES), F32))

    def far_field(waves):
        arrived = waves.finish()
        incoming = jnp.zeros((1, WAVES), F32)
        for c in range(BLOCKS):
            term = trans_ref[c : c + 1, :] * arrived[c : c + 1, :]
            incoming = incoming + jnp.where(b == c, jnp.zeros_like(term), term)

        @pl.loop(0, TILES)
        def _(tile):
            rows = rows_of(tile)
            spread = (cosine[rows, :] * incoming).astype(BF16)
            base[rows, :] = jnp.dot(spread, wave_in[...], preferred_element_type=F32)

    def fields(gbuf, use):
        buffers = (picked_a, picked_b)
        blocks = [(tile, k) for tile in range(TILES) for k in range(PER_ROW)]

        def fetch(place, turn):
            tile, k = blocks[place]
            begin = tile * TILE + turn * UNROLL
            values = [gbuf[places[(begin + step) * PER_ROW + k]].astype(F32) for step in range(UNROLL)]
            for step, value in enumerate(values):
                buffers[place % 2][pl.ds((turn * UNROLL + step) * 2, 2), :] = value

        for turn in range(TABLES):
            fetch(0, turn)
        near = jnp.zeros((TILE, COEF), F32)
        for place, (tile, k) in enumerate(blocks):
            low = buffers[place % 2][pl.ds(0, TILE, 2), :]
            high = buffers[place % 2][pl.ds(1, TILE, 2), :]
            wanted = jnp.concatenate([low, high], axis=1).astype(BF16)
            rows = pl.ds(k * ROWS + tile * TILE, TILE)
            chosen = []
            for t in range(TABLES):
                if place + 1 < len(blocks):
                    fetch(place + 1, t)
                mask = masks[t, rows, :]
                chosen.append(wanted * jnp.concatenate([mask, mask], axis=1))
            term = jnp.dot(jnp.concatenate(chosen, axis=1), padded[...], preferred_element_type=F32)
            near = near + term.astype(BF16).astype(F32)
            if k == PER_ROW - 1:
                rows = rows_of(tile)
                use(tile, mie[rows, 0:COEF] * (near + base[rows, :]))
                near = jnp.zeros((TILE, COEF), F32)

    def widened(block):
        return jnp.concatenate([block, jnp.zeros((TILE, 256 - COEF), F32)], axis=1)

    loads[0].wait()

    @pl.loop(0, TILES)
    def _(tile):
        rows = rows_of(tile)
        cosine[rows, :] = jnp.cos(angle[rows, :].astype(F32))

    loads[1].wait()
    waves_first.start(own_wave())
    first.level_one()
    for load in loads[2:]:
        load.wait()
    owners[...] = owners[...] * ROWS + near_rows[...]
    to_places = pltpu.make_async_copy(owners, places, places_sem)
    to_places.start()
    wave_in[...] = jnp.concatenate(
        [wave_in_tall[...].astype(F32), jnp.zeros((256 - COEF, WAVES), F32)], axis=0
    ).T[:, 0:COEF].astype(BF16)
    far_field(waves_first)
    first.level_two()
    padded[...] = jnp.zeros_like(padded)
    for t in range(TABLES):
        padded[t * 256 : t * 256 + COEF, :] = tables[t]
    for tile in range(TILES):
        mie[rows_of(tile), :] = turned(mie_tall[:, cols_of(tile)])
    for k in range(PER_ROW):

        @pl.loop(0, ROWS // UNROLL)
        def _(turn):
            for step in range(UNROLL):
                row = turn * UNROLL + step
                request = row * PER_ROW + k
                value = jnp.full((1, 128), table_ids[request], jnp.int32).astype(F32)
                ids_wide[pl.ds(k * ROWS + row, 1), :] = value

    @pl.loop(0, PER_ROW * TILES)
    def _(part):
        rows = rows_of(part)
        table = ids_wide[rows, :]
        for t in range(TABLES):
            masks[t, rows, :] = jnp.where(table == float(t), 1.0, 0.0).astype(BF16)

    def square(cols, sums):
        u = u_ref[:, cols]
        return (sums[0] + total(u * u),)

    (squares,) = tall_sums(square, 1)
    to_places.wait()
    first.level_three()
    first.finish()

    def use_first(tile, block):
        block = widened(block)
        narrow = block.astype(BF16)
        coded[rows_of(tile), :] = narrow
        second.store(tile, narrow)
        second.start(tile)
        b1_tall[:, cols_of(tile)] = block.T[0:COEF]

    fields(gbuf_a, use_first)

    b1_out = pltpu.make_async_copy(b1_tall, b1_hbm, out_sems.at[0])
    b1_out.start()
    waves_second.start(own_wave())

    def product(cols, sums):
        return (sums[0] + total(u_ref[:, cols] * b1_tall[:, cols]),)

    (inner,) = tall_sums(product, 1)
    slope = inner / jnp.maximum(squares, 1e-30)

    def left_over(cols, sums):
        rest = b1_tall[:, cols] - slope * u_ref[:, cols]
        return (sums[0] + total(rest * rest),)

    (left,) = tall_sums(left_over, 1)
    share_a.start(row_of(squares, inner, left, slope))
    second.level_one()
    share_b.start(row_of(*spread_stats(share_a.finish())))
    far_field(waves_second)
    second.level_two()
    squares, inner, left, slope = spread_stats(share_b.finish())
    beta_squared = squares + epsilon
    beta = jnp.sqrt(beta_squared)
    h11 = (squares - inner) / beta_squared
    rest_first = (inner + epsilon) / beta_squared
    gap = slope - rest_first
    h21 = jnp.sqrt((left + gap * gap * squares) / beta_squared + epsilon)
    scale = 1.0 / (beta * h21)
    second.level_three()
    first.drain()
    for share in (waves_first, waves_second, share_a, share_b):
        share.drain()
    second.finish()

    sums = [jnp.zeros((1, TILE), F32)] * 5

    def use_second(tile, block):
        q = widened(block).T[0:COEF]
        cols = cols_of(tile)
        q_tall[:, cols] = q
        u, b1 = u_ref[:, cols], b1_tall[:, cols]
        v = (rest_first * u - b1) * scale
        w = (rest_first * (u - b1) - (b1 - q)) * scale
        for place, pair in enumerate((u * w, v * w, w * w, u * v, v * v)):
            sums[place] = sums[place] + jnp.sum(pair, axis=0, keepdims=True)

    fields(gbuf_b, use_second)

    share_c.start(row_of(*[jnp.sum(part, axis=1, keepdims=True) for part in sums]))
    q_out = pltpu.make_async_copy(q_tall, q_hbm, out_sems.at[1])
    q_out.start()
    share_d.start(jnp.sum(share_c.finish(), axis=0, keepdims=True))
    second.drain()
    parts = jnp.sum(share_d.finish(), axis=0, keepdims=True)
    uw, vw, ww, uv, vv = (column(parts, place) for place in range(5))
    h12 = uw / beta
    h22 = vw
    left = ww + h12 * h12 * (squares / beta_squared - 2.0) + h22 * h22 * (vv - 2.0) + 2.0 * h12 * h22 * (uv / beta)
    h32 = jnp.sqrt(jnp.maximum(left, 0.0) + epsilon)
    gram_aa = h11 * h11 + h21 * h21
    gram_ab = h11 * h12 + h21 * h22
    gram_bb = h12 * h12 + h22 * h22 + h32 * h32
    rhs_first = beta * h11
    rhs_second = beta * h12
    determinant = gram_aa * gram_bb - gram_ab * gram_ab
    y1 = (gram_bb * rhs_first - gram_ab * rhs_second) / determinant
    y2 = (gram_aa * rhs_second - gram_ab * rhs_first) / determinant
    scal_ref[...] = row_of(y1 / beta, y2 * scale, rest_first)
    at_row = lax.broadcasted_iota(jnp.int32, (2, 3), 1)
    at_col = lax.broadcasted_iota(jnp.int32, (2, 3), 0)
    left_col = jnp.where(at_row == 0, h11, jnp.where(at_row == 1, h21, jnp.zeros((2, 3), F32)))
    right_col = jnp.where(at_row == 0, h12, jnp.where(at_row == 1, h22, h32))
    hess_ref[...] = jnp.where(at_col == 0, left_col, right_col)
    b1_out.wait()
    q_out.wait()
    share_c.drain()
    share_d.drain()


def combine(scal_ref, hess_in_ref, u_ref, b1_ref, q_ref, sol_ref, res_ref, hess_ref):
    scal = scal_ref[...]
    y1, y2, rest_first = (column(scal, place) for place in range(3))
    u, b1 = u_ref[...], b1_ref[...]
    sol_ref[...] = y1 * u + y2 * (rest_first * u - b1)
    image = u - b1
    res_ref[...] = u - y1 * image - y2 * (rest_first * image - (b1 - q_ref[...]))
    hess_ref[...] = hess_in_ref[...]


def body(incident, mie_coef, owner_dev, near_row, table_id, tables, wave_out, wave_in, plane_angle, far_trans):
    vmem = pl.BlockSpec(memory_space=pltpu.VMEM)
    anywhere = pl.BlockSpec(memory_space=pl.ANY)
    dma = pltpu.SemaphoreType.DMA
    u = incident[0].T
    blk_sems = [dma((BLOCKS - 1,)), dma((BLOCKS,))]
    grp_sems = [dma((GROUP - 1,)), dma((GROUP,))]
    b1, q, scal, hess = pl.pallas_call(
        kernel,
        out_shape=(
            jax.ShapeDtypeStruct((COEF, ROWS), F32),
            jax.ShapeDtypeStruct((COEF, ROWS), F32),
            jax.ShapeDtypeStruct((1, 128), F32),
            jax.ShapeDtypeStruct((2, 3), F32),
        ),
        in_specs=[anywhere] * 10,
        out_specs=(anywhere, anywhere, vmem, vmem),
        scratch_shapes=[
            pltpu.VMEM((GROUP * ROWS, 2, 128), BF16),
            pltpu.VMEM((GROUP * ROWS, 2, 128), BF16),
            pltpu.VMEM((PER_ROW * ROWS,), jnp.int32),
            pltpu.VMEM((PER_ROW * ROWS,), jnp.int32),
            pltpu.SMEM((PER_ROW * ROWS,), jnp.int32),
            pltpu.VMEM((COEF, ROWS), F32),
            pltpu.VMEM((BLOCKS, WAVES), F32),
            pltpu.SMEM((PER_ROW * ROWS,), jnp.int32),
            pltpu.VMEM((TILE * 2, 128), F32),
            pltpu.VMEM((TILE * 2, 128), F32),
            pltpu.VMEM((PER_ROW * ROWS, 128), F32),
            pltpu.VMEM((TABLES, PER_ROW * ROWS, 128), BF16),
            pltpu.VMEM((TABLES * 256, COEF), BF16),
            pltpu.VMEM((ROWS, WAVES), F32),
            pltpu.VMEM((ROWS, COEF), F32),
            pltpu.VMEM((ROWS, 256), BF16),
            pltpu.VMEM((ROWS, 256), F32),
            pltpu.VMEM((COEF, ROWS), F32),
            pltpu.VMEM((TABLES, COEF, COEF), BF16),
            pltpu.VMEM((COEF, WAVES), BF16),
            pltpu.VMEM((WAVES, COEF), BF16),
            pltpu.VMEM((COEF, WAVES), BF16),
            pltpu.VMEM((ROWS, WAVES), BF16),
            pltpu.VMEM((COEF, ROWS), F32),
            pltpu.VMEM((COEF, ROWS), F32),
            pltpu.VMEM((BLOCKS, 1, WAVES), F32),
            pltpu.VMEM((BLOCKS, 1, WAVES), F32),
            pltpu.VMEM((GROUP, 1, 128), F32),
            pltpu.VMEM((BLOCKS, 1, 128), F32),
            pltpu.VMEM((GROUP, 1, 128), F32),
            pltpu.VMEM((BLOCKS, 1, 128), F32),
            dma,
            dma((TILES,)),
            dma((9,)),
            dma((2,)),
            dma((SENDS,)),
            dma((GROUP, CHUNKS)),
            dma((SENDS,)),
            dma((GROUP, CHUNKS)),
            *blk_sems,
            *blk_sems,
            *grp_sems,
            *blk_sems,
            *grp_sems,
            *blk_sems,
        ],
        compiler_params=pltpu.CompilerParams(
            collective_id=0, has_side_effects=True, vmem_limit_bytes=56 * 2**20
        ),
    )(
        owner_dev[0, :, 0],
        near_row[0],
        table_id[0],
        u,
        mie_coef[0].T,
        tables,
        wave_out,
        wave_in.T,
        plane_angle[0],
        far_trans[0, 0],
    )
    strip = pl.BlockSpec((COEF, ROWS // 2), lambda half: (0, half))
    whole_scal = pl.BlockSpec((1, 128), lambda tile: (0, 0))
    whole_hess = pl.BlockSpec((2, 3), lambda tile: (0, 0))
    sol, res, hess = pl.pallas_call(
        combine,
        grid=(2,),
        out_shape=(
            jax.ShapeDtypeStruct((COEF, ROWS), F32),
            jax.ShapeDtypeStruct((COEF, ROWS), F32),
            jax.ShapeDtypeStruct((2, 3), F32),
        ),
        in_specs=[whole_scal, whole_hess, strip, strip, strip],
        out_specs=(strip, strip, whole_hess),
    )(scal, hess, u, b1, q)
    return sol.T[None], res.T[None], hess.T


def solution(mesh):
    return jax.shard_map(
        body,
        mesh=mesh,
        in_specs=(
            P("blk", "grp", None),
            P("blk", "grp", None),
            P("blk", "grp", None),
            P("blk", "grp"),
            P("blk", "grp"),
            P(),
            P(),
            P(),
            P("blk", "grp", None),
            P("blk", "grp", None, None),
        ),
        out_specs=(P("blk", "grp", None), P("blk", "grp", None), P()),
        check_vma=False,
    )
```

```python
import functools

import jax
import jax.numpy as jnp
from jax import lax
from jax.experimental import pallas as pl
from jax.experimental.pallas import tpu as pltpu
from jax.sharding import PartitionSpec as P

MESH = pl.DeviceIdType.MESH
F32 = jnp.float32
BF16 = jnp.bfloat16

epsilon = 1e-06

ROWS = 1024
COEF = 240
WAVES = 512
TABLES = 8
PER_ROW = 3
GROUP = 16
BLOCKS = 8
TILE = 256
TILES = ROWS // TILE
UNROLL = 32

CHUNKS = 2 * TILES
CHUNK_ROWS = tuple((tile * TILE + half * 144, (144, 112)[half]) for tile in range(TILES) for half in range(2))
Z_FIRST = (True, False) * TILES
GO_RIGHT = (True, True, False, False) * (TILES // 2)


class Gather:
    def __init__(self, gbuf, send_sems, recv_sems):
        self.gbuf, self.send_sems, self.recv_sems = gbuf, send_sems, recv_sems
        g = lax.axis_index("grp")
        self.z, self.y, self.c = g // 8, (g // 2) % 4, g % 2
        self.me = g
        self.right = self.place(0, 1)
        self.left = self.place(0, 3)
        self.across = self.place(1, 0)
        self.partner = self.place(0, 0, 1)
        self.sent = []

    def place(self, dz, dy, dc=0):
        return ((self.z + dz) % 2) * 8 + ((self.y + dy) % 4) * 2 + (self.c + dc) % 2

    def copy(self, origin, chunk, device, slot):
        begin, count = CHUNK_ROWS[chunk]
        rows = pl.ds(origin * ROWS + begin, count)
        return pltpu.make_async_remote_copy(
            src_ref=self.gbuf.at[rows],
            dst_ref=self.gbuf.at[rows],
            send_sem=self.send_sems.at[slot],
            recv_sem=self.recv_sems.at[origin, chunk],
            device_id={"grp": device},
            device_id_type=MESH,
        )

    def send(self, origin, chunk, *devices):
        for device in devices:
            copy = self.copy(origin, chunk, device, len(self.sent))
            copy.start()
            self.sent.append(copy)

    def wait(self, origin, chunk):
        self.copy(origin, chunk, self.partner, 0).wait_recv()

    def store(self, tile, coded):
        start = pl.multiple_of(self.me * ROWS + tile * TILE, TILE)
        self.gbuf[pl.ds(start, TILE)] = coded.reshape(TILE, 2, 128)

    def start(self, tile):
        for k in (2 * tile, 2 * tile + 1):
            self.send(self.me, k, self.right, self.left, self.across, self.partner)

    def level_one(self):
        last_hops = []
        for k in range(CHUNKS):
            z_first, onward = Z_FIRST[k], self.right if GO_RIGHT[k] else self.left
            for dy, from_behind in ((3, GO_RIGHT[k]), (1, not GO_RIGHT[k])):
                origin = self.place(0, dy)
                self.wait(origin, k)
                if from_behind and z_first:
                    last_hops.append((origin, k, onward))
                elif from_behind:
                    self.send(origin, k, onward)
                self.send(origin, k, *(() if z_first else (self.across,)), self.partner)
            origin = self.place(1, 0)
            self.wait(origin, k)
            if z_first:
                self.send(origin, k, onward)
                last_hops.append((origin, k, self.left if GO_RIGHT[k] else self.right))
            self.send(origin, k, self.partner)
        for origin, k, device in last_hops:
            self.send(origin, k, device)

    def level_two(self):
        self.ending = ending = []
        for k in range(CHUNKS):
            z_first, right = Z_FIRST[k], GO_RIGHT[k]
            if z_first:
                origin = self.place(1, 3 if right else 1)
                ending += [(self.place(1, 1 if right else 3), k), (self.place(0, 2), k)]
            else:
                origin = self.place(0, 2)
                ending += [(self.place(1, 3), k), (self.place(1, 1), k)]
            self.wait(origin, k)
            self.send(origin, k, (self.right if right else self.left) if z_first else self.across, self.partner)
    def level_three(self):
        for origin, k in self.ending:
            self.wait(origin, k)
            self.send(origin, k, self.partner)
        for k in range(CHUNKS):
            origin = self.place(1, 2)
            self.wait(origin, k)
            self.send(origin, k, self.partner)

    def finish(self):
        for dz in range(2):
            for dy in (0, 1, 3, 2):
                for k in range(CHUNKS):
                    self.wait(self.place(dz, dy, 1), k)

    def drain(self):
        for copy in self.sent:
            copy.wait_send()


SENDS = CHUNKS * 15


class Share:
    def __init__(self, buf, send_sems, recv_sems, axis, size):
        self.buf, self.send_sems, self.recv_sems, self.axis, self.size = buf, send_sems, recv_sems, axis, size
        self.slot = lax.axis_index(axis)

    def copy(self, source, target, step):
        return pltpu.make_async_remote_copy(
            src_ref=self.buf.at[source],
            dst_ref=self.buf.at[source],
            send_sem=self.send_sems.at[step - 1],
            recv_sem=self.recv_sems.at[source],
            device_id={self.axis: target},
            device_id_type=MESH,
        )

    def start(self, row):
        self.buf[pl.ds(self.slot, 1)] = row.reshape(1, 1, row.shape[1])
        for step in sorted(range(1, self.size), key=lambda step: -min(step % (self.size // 2), -step % (self.size // 2))):
            self.copy(self.slot, (self.slot + step) % self.size, step).start()

    def finish(self):
        for step in range(1, self.size):
            other = (self.slot + step) % self.size
            self.copy(other, other, step).wait_recv()
        return self.buf[...].reshape(self.size, self.buf.shape[2])

    def drain(self):
        for step in range(1, self.size):
            self.copy(self.slot, (self.slot + step) % self.size, step).wait_send()


def row_of(*values):
    lane = lax.broadcasted_iota(jnp.int32, (1, 128), 1)
    row = jnp.zeros((1, 128), F32)
    for place, value in enumerate(values):
        row = jnp.where(lane == place, value, row)
    return row


def column(rows, place):
    lane = lax.broadcasted_iota(jnp.int32, rows.shape, 1)
    return jnp.sum(jnp.where(lane == place, rows, 0.0), axis=1, keepdims=True)


def total(value):
    return jnp.sum(jnp.sum(value, axis=0, keepdims=True), axis=1, keepdims=True)


def spread_stats(rows):
    squares, inner, left, slope = (column(rows, place) for place in range(4))
    squares_all = jnp.sum(squares, axis=0, keepdims=True)
    inner_all = jnp.sum(inner, axis=0, keepdims=True)
    slope_all = inner_all / jnp.maximum(squares_all, 1e-30)
    gap = slope - slope_all
    left_all = jnp.sum(left + gap * gap * squares, axis=0, keepdims=True)
    return squares_all, inner_all, left_all, slope_all


def rows_of(tile):
    return pl.ds(pl.multiple_of(tile * TILE, TILE), TILE)


def cols_of(tile):
    return slice(tile * TILE, (tile + 1) * TILE)


def turned(tall):
    return jnp.concatenate([tall, jnp.zeros((256 - COEF, TILE), tall.dtype)], axis=0).T


def kernel(
    owners_hbm,
    near_rows_hbm,
    table_ids_hbm,
    u_hbm,
    mie_hbm,
    tables_hbm,
    wave_out_hbm,
    wave_in_hbm,
    angle_hbm,
    trans_hbm,
    b1_hbm,
    q_hbm,
    scal_ref,
    hess_ref,
    gbuf_a,
    gbuf_b,
    owners,
    near_rows,
    table_ids,
    u_ref,
    trans_ref,
    places,
    picked_a,
    picked_b,
    ids_wide,
    masks,
    padded,
    cosine,
    base,
    coded,
    mie,
    mie_tall,
    tables,
    wave_out,
    wave_in,
    wave_in_tall,
    angle,
    b1_tall,
    q_tall,
    wbuf_a,
    wbuf_b,
    stats_a,
    stats_b,
    stats_c,
    stats_d,
    places_sem,
    u_sems,
    in_sems,
    out_sems,
    aga_send,
    aga_recv,
    agb_send,
    agb_recv,
    wa_send,
    wa_recv,
    wb_send,
    wb_recv,
    a_send,
    a_recv,
    b_send,
    b_recv,
    c_send,
    c_recv,
    d_send,
    d_recv,
):
    g = lax.axis_index("grp")
    b = lax.axis_index("blk")
    barrier = pltpu.get_barrier_semaphore()
    for step in range(1, GROUP):
        pl.semaphore_signal(barrier, inc=1, device_id={"grp": (g + step) % GROUP}, device_id_type=MESH)
    for step in range(1, BLOCKS):
        pl.semaphore_signal(barrier, inc=1, device_id={"blk": (b + step) % BLOCKS}, device_id_type=MESH)

    tall_loads = [
        pltpu.make_async_copy(u_hbm.at[:, cols_of(tile)], u_ref.at[:, cols_of(tile)], u_sems.at[tile])
        for tile in range(TILES)
    ]
    for load in tall_loads:
        load.start()
    loads = [
        pltpu.make_async_copy(source, target, in_sems.at[place])
        for place, (source, target) in enumerate(
            (
                (angle_hbm, angle),
                (wave_out_hbm, wave_out),
                (wave_in_hbm, wave_in_tall),
                (mie_hbm, mie_tall),
                (tables_hbm, tables),
                (trans_hbm, trans_ref),
                (owners_hbm, owners),
                (near_rows_hbm, near_rows),
                (table_ids_hbm, table_ids),
            )
        )
    ]
    for load in loads:
        load.start()

    first = Gather(gbuf_a, aga_send, aga_recv)
    second = Gather(gbuf_b, agb_send, agb_recv)
    waves_first = Share(wbuf_a, wa_send, wa_recv, "blk", BLOCKS)
    waves_second = Share(wbuf_b, wb_send, wb_recv, "blk", BLOCKS)
    share_a = Share(stats_a, a_send, a_recv, "grp", GROUP)
    share_b = Share(stats_b, b_send, b_recv, "blk", BLOCKS)
    share_c = Share(stats_c, c_send, c_recv, "grp", GROUP)
    share_d = Share(stats_d, d_send, d_recv, "blk", BLOCKS)

    for tile in range(TILES):
        tall_loads[tile].wait()
        block = turned(u_ref[:, cols_of(tile)]).astype(BF16)
        coded[rows_of(tile), :] = block
        first.store(tile, block)
        if tile == 0:
            pl.semaphore_wait(barrier, GROUP + BLOCKS - 2)
        first.start(tile)

    def tall_sums(step, count):
        sums = (jnp.zeros((1, 1), F32),) * count
        for tile in range(TILES):
            sums = step(cols_of(tile), sums)
        return sums

    def own_wave():
        def step(tile, wave):
            rows = rows_of(tile)
            outgoing = jnp.dot(coded[rows, 0:COEF], wave_out[...], preferred_element_type=F32)
            return wave + jnp.sum(cosine[rows, :] * outgoing, axis=0, keepdims=True)

        return lax.fori_loop(0, TILES, step, jnp.zeros((1, WAVES), F32))

    def far_field(waves):
        arrived = waves.finish()
        incoming = jnp.zeros((1, WAVES), F32)
        for c in range(BLOCKS):
            term = trans_ref[c : c + 1, :] * arrived[c : c + 1, :]
            incoming = incoming + jnp.where(b == c, jnp.zeros_like(term), term)

        @pl.loop(0, TILES)
        def _(tile):
            rows = rows_of(tile)
            spread = (cosine[rows, :] * incoming).astype(BF16)
            base[rows, :] = jnp.dot(spread, wave_in[...], preferred_element_type=F32)

    def fields(gbuf, use):
        buffers = (picked_a, picked_b)
        blocks = [(tile, k) for tile in range(TILES) for k in range(PER_ROW)]

        def fetch(place, turn):
            tile, k = blocks[place]
            begin = tile * TILE + turn * UNROLL
            values = [gbuf[places[(begin + step) * PER_ROW + k]].astype(F32) for step in range(UNROLL)]
            for step, value in enumerate(values):
                buffers[place % 2][pl.ds((turn * UNROLL + step) * 2, 2), :] = value

        for turn in range(TABLES):
            fetch(0, turn)
        near = jnp.zeros((TILE, COEF), F32)
        for place, (tile, k) in enumerate(blocks):
            low = buffers[place % 2][pl.ds(0, TILE, 2), :]
            high = buffers[place % 2][pl.ds(1, TILE, 2), :]
            wanted = jnp.concatenate([low, high], axis=1).astype(BF16)
            rows = pl.ds(k * ROWS + tile * TILE, TILE)
            chosen = []
            for t in range(TABLES):
                if place + 1 < len(blocks):
                    fetch(place + 1, t)
                mask = masks[t, rows, :]
                chosen.append(wanted * jnp.concatenate([mask, mask], axis=1))
            term = jnp.dot(jnp.concatenate(chosen, axis=1), padded[...], preferred_element_type=F32)
            near = near + term.astype(BF16).astype(F32)
            if k == PER_ROW - 1:
                rows = rows_of(tile)
                use(tile, mie[rows, 0:COEF] * (near + base[rows, :]))
                near = jnp.zeros((TILE, COEF), F32)

    def widened(block):
        return jnp.concatenate([block, jnp.zeros((TILE, 256 - COEF), F32)], axis=1)

    loads[0].wait()

    @pl.loop(0, TILES)
    def _(tile):
        rows = rows_of(tile)
        cosine[rows, :] = jnp.cos(angle[rows, :].astype(F32))

    loads[1].wait()
    waves_first.start(own_wave())
    first.level_one()
    for load in loads[2:]:
        load.wait()
    owners[...] = owners[...] * ROWS + near_rows[...]
    to_places = pltpu.make_async_copy(owners, places, places_sem)
    to_places.start()
    wave_in[...] = jnp.concatenate(
        [wave_in_tall[...].astype(F32), jnp.zeros((256 - COEF, WAVES), F32)], axis=0
    ).T[:, 0:COEF].astype(BF16)
    far_field(waves_first)
    first.level_two()
    padded[...] = jnp.zeros_like(padded)
    for t in range(TABLES):
        padded[t * 256 : t * 256 + COEF, :] = tables[t]
    for tile in range(TILES):
        mie[rows_of(tile), :] = turned(mie_tall[:, cols_of(tile)])
    for k in range(PER_ROW):

        @pl.loop(0, ROWS // UNROLL)
        def _(turn):
            for step in range(UNROLL):
                row = turn * UNROLL + step
                request = row * PER_ROW + k
                value = jnp.full((1, 128), table_ids[request], jnp.int32).astype(F32)
                ids_wide[pl.ds(k * ROWS + row, 1), :] = value

    @pl.loop(0, PER_ROW * TILES)
    def _(part):
        rows = rows_of(part)
        table = ids_wide[rows, :]
        for t in range(TABLES):
            masks[t, rows, :] = jnp.where(table == float(t), 1.0, 0.0).astype(BF16)

    def square(cols, sums):
        u = u_ref[:, cols]
        return (sums[0] + total(u * u),)

    (squares,) = tall_sums(square, 1)
    to_places.wait()
    first.level_three()
    first.finish()

    def use_first(tile, block):
        block = widened(block)
        narrow = block.astype(BF16)
        coded[rows_of(tile), :] = narrow
        second.store(tile, narrow)
        second.start(tile)
        b1_tall[:, cols_of(tile)] = block.T[0:COEF]

    fields(gbuf_a, use_first)

    b1_out = pltpu.make_async_copy(b1_tall, b1_hbm, out_sems.at[0])
    b1_out.start()
    waves_second.start(own_wave())

    def product(cols, sums):
        return (sums[0] + total(u_ref[:, cols] * b1_tall[:, cols]),)

    (inner,) = tall_sums(product, 1)
    slope = inner / jnp.maximum(squares, 1e-30)

    def left_over(cols, sums):
        rest = b1_tall[:, cols] - slope * u_ref[:, cols]
        return (sums[0] + total(rest * rest),)

    (left,) = tall_sums(left_over, 1)
    share_a.start(row_of(squares, inner, left, slope))
    second.level_one()
    share_b.start(row_of(*spread_stats(share_a.finish())))
    far_field(waves_second)
    second.level_two()
    squares, inner, left, slope = spread_stats(share_b.finish())
    beta_squared = squares + epsilon
    beta = jnp.sqrt(beta_squared)
    h11 = (squares - inner) / beta_squared
    rest_first = (inner + epsilon) / beta_squared
    gap = slope - rest_first
    h21 = jnp.sqrt((left + gap * gap * squares) / beta_squared + epsilon)
    scale = 1.0 / (beta * h21)
    second.level_three()
    first.drain()
    for share in (waves_first, waves_second, share_a, share_b):
        share.drain()
    second.finish()

    sums = [jnp.zeros((1, TILE), F32)] * 3

    def use_second(tile, block):
        q = widened(block).T[0:COEF]
        cols = cols_of(tile)
        q_tall[:, cols] = q
        u, b1 = u_ref[:, cols], b1_tall[:, cols]
        v = (rest_first * u - b1) * scale
        w = (rest_first * (u - b1) - (b1 - q)) * scale
        for place, pair in enumerate((u * w, v * w, w * w)):
            sums[place] = sums[place] + jnp.sum(pair, axis=0, keepdims=True)

    fields(gbuf_b, use_second)

    share_c.start(row_of(*[jnp.sum(part, axis=1, keepdims=True) for part in sums]))
    q_out = pltpu.make_async_copy(q_tall, q_hbm, out_sems.at[1])
    q_out.start()
    share_d.start(jnp.sum(share_c.finish(), axis=0, keepdims=True))
    second.drain()
    parts = jnp.sum(share_d.finish(), axis=0, keepdims=True)
    uw, vw, ww = (column(parts, place) for place in range(3))
    uv = epsilon * (squares - inner) / beta_squared * scale
    vv = (left + gap * gap * squares) * (scale * scale)
    h12 = uw / beta
    h22 = vw
    left = ww + h12 * h12 * (squares / beta_squared - 2.0) + h22 * h22 * (vv - 2.0) + 2.0 * h12 * h22 * (uv / beta)
    h32 = jnp.sqrt(jnp.maximum(left, 0.0) + epsilon)
    gram_aa = h11 * h11 + h21 * h21
    gram_ab = h11 * h12 + h21 * h22
    gram_bb = h12 * h12 + h22 * h22 + h32 * h32
    rhs_first = beta * h11
    rhs_second = beta * h12
    determinant = gram_aa * gram_bb - gram_ab * gram_ab
    y1 = (gram_bb * rhs_first - gram_ab * rhs_second) / determinant
    y2 = (gram_aa * rhs_second - gram_ab * rhs_first) / determinant
    scal_ref[...] = row_of(y1 / beta, y2 * scale, rest_first)
    at_row = lax.broadcasted_iota(jnp.int32, (2, 3), 1)
    at_col = lax.broadcasted_iota(jnp.int32, (2, 3), 0)
    left_col = jnp.where(at_row == 0, h11, jnp.where(at_row == 1, h21, jnp.zeros((2, 3), F32)))
    right_col = jnp.where(at_row == 0, h12, jnp.where(at_row == 1, h22, h32))
    hess_ref[...] = jnp.where(at_col == 0, left_col, right_col)
    b1_out.wait()
    q_out.wait()
    share_c.drain()
    share_d.drain()


def combine(scal_ref, hess_in_ref, u_ref, b1_ref, q_ref, sol_ref, res_ref, hess_ref):
    scal = scal_ref[...]
    y1, y2, rest_first = (column(scal, place) for place in range(3))
    u, b1 = u_ref[...], b1_ref[...]
    sol_ref[...] = y1 * u + y2 * (rest_first * u - b1)
    image = u - b1
    res_ref[...] = u - y1 * image - y2 * (rest_first * image - (b1 - q_ref[...]))
    hess_ref[...] = hess_in_ref[...]


def body(incident, mie_coef, owner_dev, near_row, table_id, tables, wave_out, wave_in, plane_angle, far_trans):
    vmem = pl.BlockSpec(memory_space=pltpu.VMEM)
    anywhere = pl.BlockSpec(memory_space=pl.ANY)
    dma = pltpu.SemaphoreType.DMA
    u = incident[0].T
    blk_sems = [dma((BLOCKS - 1,)), dma((BLOCKS,))]
    grp_sems = [dma((GROUP - 1,)), dma((GROUP,))]
    b1, q, scal, hess = pl.pallas_call(
        kernel,
        out_shape=(
            jax.ShapeDtypeStruct((COEF, ROWS), F32),
            jax.ShapeDtypeStruct((COEF, ROWS), F32),
            jax.ShapeDtypeStruct((1, 128), F32),
            jax.ShapeDtypeStruct((2, 3), F32),
        ),
        in_specs=[anywhere] * 10,
        out_specs=(anywhere, anywhere, vmem, vmem),
        scratch_shapes=[
            pltpu.VMEM((GROUP * ROWS, 2, 128), BF16),
            pltpu.VMEM((GROUP * ROWS, 2, 128), BF16),
            pltpu.VMEM((PER_ROW * ROWS,), jnp.int32),
            pltpu.VMEM((PER_ROW * ROWS,), jnp.int32),
            pltpu.SMEM((PER_ROW * ROWS,), jnp.int32),
            pltpu.VMEM((COEF, ROWS), F32),
            pltpu.VMEM((BLOCKS, WAVES), F32),
            pltpu.SMEM((PER_ROW * ROWS,), jnp.int32),
            pltpu.VMEM((TILE * 2, 128), F32),
            pltpu.VMEM((TILE * 2, 128), F32),
            pltpu.VMEM((PER_ROW * ROWS, 128), F32),
            pltpu.VMEM((TABLES, PER_ROW * ROWS, 128), BF16),
            pltpu.VMEM((TABLES * 256, COEF), BF16),
            pltpu.VMEM((ROWS, WAVES), F32),
            pltpu.VMEM((ROWS, COEF), F32),
            pltpu.VMEM((ROWS, 256), BF16),
            pltpu.VMEM((ROWS, 256), F32),
            pltpu.VMEM((COEF, ROWS), F32),
            pltpu.VMEM((TABLES, COEF, COEF), BF16),
            pltpu.VMEM((COEF, WAVES), BF16),
            pltpu.VMEM((WAVES, COEF), BF16),
            pltpu.VMEM((COEF, WAVES), BF16),
            pltpu.VMEM((ROWS, WAVES), BF16),
            pltpu.VMEM((COEF, ROWS), F32),
            pltpu.VMEM((COEF, ROWS), F32),
            pltpu.VMEM((BLOCKS, 1, WAVES), F32),
            pltpu.VMEM((BLOCKS, 1, WAVES), F32),
            pltpu.VMEM((GROUP, 1, 128), F32),
            pltpu.VMEM((BLOCKS, 1, 128), F32),
            pltpu.VMEM((GROUP, 1, 128), F32),
            pltpu.VMEM((BLOCKS, 1, 128), F32),
            dma,
            dma((TILES,)),
            dma((9,)),
            dma((2,)),
            dma((SENDS,)),
            dma((GROUP, CHUNKS)),
            dma((SENDS,)),
            dma((GROUP, CHUNKS)),
            *blk_sems,
            *blk_sems,
            *grp_sems,
            *blk_sems,
            *grp_sems,
            *blk_sems,
        ],
        compiler_params=pltpu.CompilerParams(
            collective_id=0, has_side_effects=True, vmem_limit_bytes=56 * 2**20
        ),
    )(
        owner_dev[0, :, 0],
        near_row[0],
        table_id[0],
        u,
        mie_coef[0].T,
        tables,
        wave_out,
        wave_in.T,
        plane_angle[0],
        far_trans[0, 0],
    )
    strip = pl.BlockSpec((COEF, ROWS // 2), lambda half: (0, half))
    whole_scal = pl.BlockSpec((1, 128), lambda tile: (0, 0))
    whole_hess = pl.BlockSpec((2, 3), lambda tile: (0, 0))
    sol, res, hess = pl.pallas_call(
        combine,
        grid=(2,),
        out_shape=(
            jax.ShapeDtypeStruct((COEF, ROWS), F32),
            jax.ShapeDtypeStruct((COEF, ROWS), F32),
            jax.ShapeDtypeStruct((2, 3), F32),
        ),
        in_specs=[whole_scal, whole_hess, strip, strip, strip],
        out_specs=(strip, strip, whole_hess),
    )(scal, hess, u, b1, q)
    return sol.T[None], res.T[None], hess.T


def solution(mesh):
    return jax.shard_map(
        body,
        mesh=mesh,
        in_specs=(
            P("blk", "grp", None),
            P("blk", "grp", None),
            P("blk", "grp", None),
            P("blk", "grp"),
            P("blk", "grp"),
            P(),
            P(),
            P(),
            P("blk", "grp", None),
            P("blk", "grp", None, None),
        ),
        out_specs=(P("blk", "grp", None), P("blk", "grp", None), P()),
        check_vma=False,
    )
```
